32 devices in a mesh: lat: 4 (over y, x), lon: 8 (over z, core).
Axes of the slice: x: 2, y: 2, z: 4, core: 2. Of those that a mesh axis runs over, the one named last changes fastest.
Arguments:
- inputs: bfloat16 [360, 360, 256], P('lat', 'lon'), may hold values from -6 to 6
- kernel: bfloat16 [3, 3, 256, 256], replicated, may hold values from -0.125 to 0.125
- cotangent: bfloat16 [360, 360, 256], P('lat', 'lon'), may hold values from -6 to 6
Outputs:
- outputs: bfloat16 [360, 360, 256], P('lat', 'lon')
- input_grad: bfloat16 [360, 360, 256], P('lat', 'lon')
- kernel_grad: float32 [3, 3, 256, 256], replicated
The draws below stay inside these ranges and needn't reach their ends.
All inputs are finite; a program needn't handle non-finite values.
Results may differ from the reference program's by a relative error of at most 0.001.
Values may be sent and summed in bfloat16 or wider, within the bound.
No kernel may reach another device: no remote copies, remote signals or barrier semaphores. Data moves between devices by JAX's collectives and lax.ppermute only.
A program may use at most 192 MiB of HBM per device.

```python
import math
import jax
import jax.numpy as jnp

CH = 256
NLAT = 360
NLON = 360


def steps_of(stream_key, shape, shards, least, top_value):
    factor_of = 1.0
    for position, parts in shards:
        heights = jax.random.uniform(jax.random.fold_in(jax.random.fold_in(stream_key, 6), position), (parts,), jnp.float32, least / len(shards), top_value / len(shards))
        factor_of = factor_of * jnp.repeat(jnp.exp(heights), shape[position] // parts).reshape((-1,) + (1,) * (len(shape) - 1 - position))
    return factor_of


def centred(key, shape, scale, limit, pieces=(), dtype=jnp.bfloat16):
    loudness = steps_of(key, shape, pieces, -0.22, 0.18) if pieces else 1.0
    values = jax.random.normal(key, shape, jnp.float32) * scale * loudness
    return jnp.minimum(jnp.maximum(values, -limit), limit).astype(dtype)


def setup_inputs(seed: int = 0) -> dict:
    splits = jax.random.split(jax.random.key(seed), 4)
    inputs = centred(splits[0], (NLAT, NLON, CH), 1.0, 6.0, ((0, 4), (1, 8)))
    kernel = centred(splits[1], (3, 3, CH, CH), (9 * CH) ** -0.5, 0.125)
    cotangent = centred(splits[2], (NLAT, NLON, CH), 1.0, 6.0, ((0, 4), (1, 8)))
    return dict(inputs=inputs, kernel=kernel, cotangent=cotangent)


def pole_pad(field):
    half = NLON // 2
    top = jnp.roll(field[0], -half, axis=0)[None]
    bottom = jnp.roll(field[-1], -half, axis=0)[None]
    rows = jnp.concatenate([top, field, bottom], 0)
    return jnp.concatenate([rows[:, -1:], rows, rows[:, :1]], 1)

def reference(inputs, kernel, cotangent):
    padded = pole_pad(inputs)
    flat_grad = cotangent.reshape(-1, CH)
    result = jnp.zeros((NLAT * NLON, CH), jnp.float32)
    pad_grad = jnp.zeros((NLAT + 2, NLON + 2, CH), jnp.float32)
    taps = []
    for row_tap in range(3):
        for col_tap in range(3):
            window = padded[row_tap:row_tap + NLAT, col_tap:col_tap + NLON].reshape(-1, CH)
            result = result + jnp.dot(window, kernel[row_tap, col_tap], preferred_element_type=jnp.float32)
            taps.append(jnp.dot(window.T, flat_grad, preferred_element_type=jnp.float32))
            spread = jnp.dot(flat_grad, kernel[row_tap, col_tap].T, preferred_element_type=jnp.float32)
            pad_grad = pad_grad.at[row_tap:row_tap + NLAT, col_tap:col_tap + NLON].add(spread.reshape(NLAT, NLON, CH))
    outputs = result.reshape(NLAT, NLON, CH).astype(jnp.bfloat16)
    kernel_grad = jnp.stack(taps).reshape(3, 3, CH, CH) * (1.0 / math.sqrt(NLAT * NLON))
    inner = pad_grad[:, 1:-1]
    inner = inner.at[:, -1].add(pad_grad[:, 0])
    inner = inner.at[:, 0].add(pad_grad[:, -1])
    half = NLON // 2
    grad = inner[1:-1]
    grad = grad.at[0].add(jnp.roll(inner[0], half, axis=0))
    grad = grad.at[-1].add(jnp.roll(inner[-1], half, axis=0))
    return (outputs, grad.astype(jnp.bfloat16), kernel_grad)
```

```python
import functools
import math

import jax
import jax.numpy as jnp
from jax import lax
from jax.experimental import pallas as pl
from jax.experimental.pallas import tpu as pltpu
from jax.sharding import PartitionSpec as P

F32 = jnp.float32
BF16 = jnp.bfloat16
VMEM = pl.BlockSpec(memory_space=pltpu.VMEM)
SMEM = pl.BlockSpec(memory_space=pltpu.SMEM)
HBM = pl.BlockSpec(memory_space=pltpu.HBM)


def padded_width(cols):
    return -(-(cols + 3) // 16) * 16


def params(mib):
    return pltpu.CompilerParams(vmem_limit_bytes=mib << 20)


def shifted(row, left, right, wide):
    cols, width = row.shape
    middle = jnp.zeros((wide - cols - 2, width), F32)
    base = jnp.concatenate([row.astype(F32), right, middle, left], 0)
    return (
        pltpu.roll(base, 1, 0).astype(BF16),
        base.astype(BF16),
        pltpu.roll(base, wide - 1, 0).astype(BF16),
    )


def fill_window(field, ends, sides, side_rows, window, first, rows):
    total, cols, width = field.shape
    wide = padded_width(cols)
    side_rows[...] = sides[...].astype(F32)

    def put(slot, row, at):
        parts = shifted(row, side_rows[0, pl.ds(at, 1)], side_rows[1, pl.ds(at, 1)], wide)
        start = slot * wide if isinstance(slot, int) else pl.multiple_of(slot * wide, 16)
        for tap, part in enumerate(parts):
            window[pl.ds(start, wide), tap * width : (tap + 1) * width] = part

    low = 0
    if first == 0:
        put(0, ends[0], 0)
        low = 1
    high = rows + 2
    if first + rows == total:
        put(rows + 1, ends[1], total + 1)
        high = rows + 1

    @pl.loop(low, high)
    def _(slot):
        put(slot, field[first + slot - 1], first + slot)


def block_rows(rows):
    return max(n for n in range(1, 6) if rows % n == 0)


def conv_kernel(taps, field, ends, sides, weights, out, window, side_rows, result, sem, *, first, rows):
    total, cols, width = field.shape
    wide = padded_width(cols)
    fill_window(field, ends, sides, side_rows, window, first, rows)
    step = block_rows(rows)

    def rows_of(start, count, which):
        acc = None
        for a in range(3):
            at = start + a
            at = at * wide if isinstance(at, int) else pl.multiple_of(at * wide, 16)
            term = jnp.dot(window[pl.ds(at, count * wide), :], weights[which[a]], preferred_element_type=F32)
            acc = term if acc is None else acc + term
        return acc.reshape(count, wide, width)[:, :cols].astype(BF16)

    @pl.loop(0, rows // step)
    def _(i):
        result[pl.ds(i * step, step)] = rows_of(i * step, step, (0, 1, 2))

    if first == 0:
        result[0:1] = rows_of(0, 1, (taps[0], 1, 2))
    if first + rows == total:
        result[rows - 1 : rows] = rows_of(rows - 1, 1, (0, 1, taps[1]))
    copy = pltpu.make_async_copy(result, out, sem)
    copy.start()
    copy.wait()


def conv(taps, field, ends, sides, weights, first, rows):
    total, cols, width = field.shape
    wide = padded_width(cols)
    return pl.pallas_call(
        functools.partial(conv_kernel, first=first, rows=rows),
        out_shape=jax.ShapeDtypeStruct((rows, cols, width), BF16),
        in_specs=[SMEM, VMEM, VMEM, VMEM, VMEM],
        out_specs=HBM,
        scratch_shapes=[
            pltpu.VMEM(((rows + 2) * wide, 3 * width), BF16),
            pltpu.VMEM((2, total + 2, width), F32),
            pltpu.VMEM((rows, cols, width), BF16),
            pltpu.SemaphoreType.DMA,
        ],
        compiler_params=params(24),
        cost_estimate=pl.CostEstimate(
            flops=18 * rows * wide * width * width, bytes_accessed=4 * rows * wide * width, transcendentals=0
        ),
    )(taps, field, ends, sides, weights)


def weight_kernel(half, field, cot, ends, sides, send, keep, window, side_rows, turned, tap_out):
    total, cols, width = field.shape
    wide = padded_width(cols)
    fill_window(field, ends, sides, side_rows, window, 0, total)
    blank = jnp.zeros((wide - cols, width), F32)
    group = 128 // math.gcd(128, wide)
    span = group * wide

    def chunk(start, count):
        return [part for j in range(count) for part in (cot[start + j].astype(F32), blank)]

    @pl.loop(0, total // group)
    def _(i):
        value = jnp.concatenate(chunk(i * group, group), 0)
        turned[:, pl.ds(pl.multiple_of(i * span, 128), span)] = value.T.astype(BF16)

    rest = total % group
    if rest:
        start = total - rest
        value = jnp.concatenate(chunk(start, rest) + [jnp.zeros((span - rest * wide, width), F32)], 0)
        turned[:, start * wide : start * wide + span] = value.T.astype(BF16)
    mine = half[0]
    part = width // 2
    for a in range(3):
        value = jnp.dot(
            turned[:, : total * wide],
            window[a * wide : (a + total) * wide, :],
            preferred_element_type=F32,
        )
        for b in range(3):
            tap = 3 * a + b
            tap_out[tap] = value[:, b * width : (b + 1) * width].T
            keep[tap * part : (tap + 1) * part] = tap_out[tap, pl.ds(pl.multiple_of(mine * part, part), part)]
            send[tap * part : (tap + 1) * part] = tap_out[tap, pl.ds(pl.multiple_of((1 - mine) * part, part), part)]


def weight_terms(half, field, cot, ends, sides):
    total, cols, width = field.shape
    wide = padded_width(cols)
    group = 128 // math.gcd(128, wide)
    shape = jax.ShapeDtypeStruct((9 * width // 2, width), F32)
    return pl.pallas_call(
        weight_kernel,
        out_shape=(shape, shape),
        in_specs=[SMEM, VMEM, VMEM, VMEM, VMEM],
        out_specs=(VMEM, VMEM),
        scratch_shapes=[
            pltpu.VMEM(((total + 2) * wide, 3 * width), BF16),
            pltpu.VMEM((2, total + 2, width), F32),
            pltpu.VMEM((width, -(-total // group) * group * wide), BF16),
            pltpu.VMEM((9, width, width), F32),
        ],
        compiler_params=params(32),
        cost_estimate=pl.CostEstimate(
            flops=18 * total * wide * width * width, bytes_accessed=4 * total * wide * width, transcendentals=0
        ),
    )(half, field, cot, ends, sides)


def add_blocks(places, terms, blocks, scale=None):
    rows, width = terms[0].shape
    size = rows // blocks
    count = len(places)
    order = jnp.stack(places).astype(jnp.int32)

    def body(where, *refs):
        sources, outs = refs[: len(terms)], refs[len(terms) :]
        for k in range(count):
            at = pl.ds(pl.multiple_of(where[k] * size, 8), size)
            value = sources[0][at]
            for source in sources[1:]:
                value = value + source[at]
            outs[k][...] = value if scale is None else value * scale

    shape = jax.ShapeDtypeStruct((size, width), F32)
    return pl.pallas_call(
        body,
        out_shape=(shape,) * count,
        in_specs=[SMEM] + [VMEM] * len(terms),
        out_specs=(VMEM,) * count,
        compiler_params=params(8),
        cost_estimate=pl.CostEstimate(
            flops=rows * width, bytes_accessed=4 * rows * width * (len(terms) + 1), transcendentals=0
        ),
    )(order, *terms)


def lay_out(places, parts):
    size, width = parts[0].shape
    order = jnp.stack(places).astype(jnp.int32)

    def body(where, *refs):
        for k in range(len(parts)):
            refs[-1][pl.ds(pl.multiple_of(where[k] * size, 8), size)] = refs[k][...]

    return pl.pallas_call(
        body,
        out_shape=jax.ShapeDtypeStruct((size * len(parts), width), F32),
        in_specs=[SMEM] + [VMEM] * len(parts),
        out_specs=VMEM,
        compiler_params=params(8),
        cost_estimate=pl.CostEstimate(
            flops=0, bytes_accessed=8 * size * width * len(parts), transcendentals=0
        ),
    )(order, *parts)


def finish(half, own, other):
    rows, width = own.shape
    part = width // 2
    shape = (rows // part, part, width)

    def body(mine, own, other, out, sems):
        at = mine[0]
        copies = [
            pltpu.make_async_copy(own, out.at[:, at], sems.at[0]),
            pltpu.make_async_copy(other, out.at[:, 1 - at], sems.at[1]),
        ]
        for copy in copies:
            copy.start()
        for copy in copies:
            copy.wait()

    out = pl.pallas_call(
        body,
        out_shape=jax.ShapeDtypeStruct((rows // part, 2, part, width), F32),
        in_specs=[SMEM, VMEM, VMEM],
        out_specs=HBM,
        scratch_shapes=[pltpu.SemaphoreType.DMA((2,))],
        compiler_params=params(8),
    )(half, own.reshape(shape), other.reshape(shape))
    return out.reshape(3, 3, width, width)


def swap(value, axis, mask):
    count = lax.axis_size(axis)
    return lax.ppermute(value, axis, [(i, i ^ mask) for i in range(count)])


def swap_next(value, axis):
    count = lax.axis_size(axis)
    return lax.ppermute(value, axis, [(i, (i + (1 if i % 2 else -1)) % count) for i in range(count)])


def swap_rows(value):
    bands, sectors = lax.axis_size("lat"), lax.axis_size("lon")
    pairs = []
    for band in range(bands):
        for sector in range(sectors):
            if band == 0 or band == bands - 1:
                other = (band, (sector + sectors // 2) % sectors)
            else:
                other = (band + (1 if band % 2 else -1), sector)
            pairs.append((band * sectors + sector, other[0] * sectors + other[1]))
    return lax.ppermute(value, ("lat", "lon"), pairs)


def halos(inputs, cotangent):
    even_band = lax.axis_index("lat") % 2 == 0
    even_sector = lax.axis_index("lon") % 2 == 0
    first = jnp.stack([inputs[0], cotangent[0]])
    last = jnp.stack([inputs[-1], cotangent[-1]])
    near = swap(jnp.where(even_band, last, first), "lat", 1)
    far = swap_rows(jnp.where(even_band, first, last))
    top = jnp.where(even_band, far, near)
    bottom = jnp.where(even_band, near, far)
    ends = jnp.stack([top, bottom], 1)

    def side(column):
        return jnp.stack(
            [
                jnp.concatenate([ends[k, :1, column], field[:, column], ends[k, 1:, column]], 0)
                for k, field in enumerate((inputs, cotangent))
            ]
        )

    first, last = side(0), side(-1)
    near = swap(jnp.where(even_sector, last, first), "lon", 1)
    far = swap_next(jnp.where(even_sector, first, last), "lon")
    left = jnp.where(even_sector, far, near)
    right = jnp.where(even_sector, near, far)
    sides = jnp.stack([left, right], 1)
    return ends, sides


def local(inputs, kernel, cotangent):
    rows, cols, width = inputs.shape
    bands, sectors = lax.axis_size("lat"), lax.axis_size("lon")
    band, sector = lax.axis_index("lat"), lax.axis_index("lon")
    ends, sides = halos(inputs, cotangent)
    half = (sector % 2).astype(jnp.int32)[None]
    send, keep = weight_terms(half, inputs, cotangent, ends[0], sides[0])

    got = swap(send, "lon", 1)
    parts = add_blocks([band ^ m for m in range(bands)], [keep, got], bands)
    got = [swap(parts[m], "lat", m) for m in range(1, bands)]
    place = (sector // 2) % 2
    keep, send = add_blocks([place, 1 - place], [parts[0], *got], 2)
    got = swap(send, "lon", 2)
    factor = 1.0 / math.sqrt(rows * cols * bands * sectors)
    mask = 4
    terms = [keep, got]
    zero = jnp.int32(0)
    while mask < sectors:
        (value,) = add_blocks([zero], terms, 1)
        terms = [value, swap(value, "lon", mask)]
        mask *= 2
    (value,) = add_blocks([zero], terms, 1, factor)
    got = swap(value, "lon", 2)
    value = lay_out([place, 1 - place], [value, got])
    got = [swap(value, "lat", m) for m in range(1, bands)]
    value = lay_out([band ^ m for m in range(bands)], [value, *got])
    got = swap(value, "lon", 1)
    kernel_grad = finish(half, value, got)

    weights = kernel.reshape(3, 3 * width, width)
    flipped = jnp.transpose(kernel[::-1, ::-1], (0, 1, 3, 2)).reshape(3, 3 * width, width)
    plain = jnp.array([0, 2], jnp.int32)
    poles = jnp.stack([jnp.where(band == 0, 2, 0), jnp.where(band == bands - 1, 0, 2)]).astype(jnp.int32)
    outputs = conv(plain, inputs, ends[0], sides[0], weights, 0, rows)
    input_grad = conv(poles, cotangent, ends[1], sides[1], flipped, 0, rows)
    return (outputs, input_grad, kernel_grad)


def solution(mesh):
    in_specs = (P("lat", "lon", None), P(), P("lat", "lon", None))
    out_specs = (P("lat", "lon", None), P("lat", "lon", None), P())
    return jax.shard_map(local, mesh=mesh, in_specs=in_specs, out_specs=out_specs, check_vma=False)
```

```python
import math

import jax
import jax.numpy as jnp
from jax import lax
from jax.experimental import pallas as pl
from jax.experimental.pallas import tpu as pltpu
from jax.sharding import PartitionSpec as P


F32 = jnp.float32
BF16 = jnp.bfloat16
HALF = jnp.float16
VMEM = pl.BlockSpec(memory_space=pltpu.VMEM)
SMEM = pl.BlockSpec(memory_space=pltpu.SMEM)
HBM = pl.BlockSpec(memory_space=pltpu.HBM)


def padded_width(cols):
    return -(-(cols + 3) // 16) * 16


def params(mib):
    return pltpu.CompilerParams(vmem_limit_bytes=mib << 20)


def shifted(row, left, right, wide):
    cols, width = row.shape
    middle = jnp.zeros((wide - cols - 2, width), F32)
    base = jnp.concatenate([row.astype(F32), right, middle, left], 0)
    return (
        pltpu.roll(base, 1, 0).astype(BF16),
        base.astype(BF16),
        pltpu.roll(base, wide - 1, 0).astype(BF16),
    )


def fill_window(field, ends, sides, side_rows, window, first, rows):
    total, cols, width = field.shape
    wide = padded_width(cols)
    side_rows[...] = sides[...].astype(F32)

    def put(slot, row, at):
        parts = shifted(row, side_rows[0, pl.ds(at, 1)], side_rows[1, pl.ds(at, 1)], wide)
        start = slot * wide if isinstance(slot, int) else pl.multiple_of(slot * wide, 16)
        for tap, part in enumerate(parts):
            window[pl.ds(start, wide), tap * width : (tap + 1) * width] = part

    low = 0
    if first == 0:
        put(0, ends[0], 0)
        low = 1
    high = rows + 2
    if first + rows == total:
        put(rows + 1, ends[1], total + 1)
        high = rows + 1

    @pl.loop(low, high)
    def _(slot):
        put(slot, field[first + slot - 1], first + slot)


def block_rows(rows):
    return max(n for n in range(1, 6) if rows % n == 0)


def conv_rows(taps, window, weights, result, out, sem, cols, first, rows, total):
    width = weights.shape[-1]
    wide = padded_width(cols)
    step = block_rows(rows)

    def rows_of(start, count, which):
        acc = None
        for a in range(3):
            at = start + a
            at = at * wide if isinstance(at, int) else pl.multiple_of(at * wide, 16)
            term = jnp.dot(window[pl.ds(at, count * wide), :], weights[which[a]], preferred_element_type=F32)
            acc = term if acc is None else acc + term
        return acc.reshape(count, wide, width)[:, :cols].astype(BF16)

    def write(at):
        return pltpu.make_async_copy(result.at[pl.ds(at, step)], out.at[pl.ds(first + at, step)], sem)

    count = rows // step
    low = int(first == 0 and taps is not None)
    high = count - int(first + rows == total and taps is not None)

    @pl.loop(low, high)
    def _(i):
        result[pl.ds(i * step, step)] = rows_of(i * step, step, (0, 1, 2))
        write(i * step).start()

    if low:
        result[0:step] = rows_of(0, step, (0, 1, 2))
        result[0:1] = rows_of(0, 1, (taps[0], 1, 2))
        write(0).start()
    if high < count:
        result[rows - step : rows] = rows_of(rows - step, step, (0, 1, 2))
        result[rows - 1 : rows] = rows_of(rows - 1, 1, (0, 1, taps[1]))
        write(rows - step).start()
    pltpu.make_async_copy(result, out.at[pl.ds(first, rows)], sem).wait()


def conv_cost(rows, cols, width):
    wide = padded_width(cols)
    return pl.CostEstimate(
        flops=18 * rows * wide * width * width, bytes_accessed=4 * rows * wide * width, transcendentals=0
    )


def backward(taps, field, ends, sides, weights, first, rows, out=None):
    total, cols, width = field.shape
    wide = padded_width(cols)
    more = [] if out is None else [out]

    def body(taps, field, ends, sides, weights, *rest):
        out, window, side_rows, result, sem = rest[-5:]
        fill_window(field, ends, sides, side_rows, window, first, rows)
        conv_rows(taps, window, weights, result, out, sem, cols, first, rows, total)

    return pl.pallas_call(
        body,
        out_shape=jax.ShapeDtypeStruct((total, cols, width), BF16),
        in_specs=[SMEM, VMEM, VMEM, VMEM, VMEM] + [HBM] * len(more),
        out_specs=HBM,
        scratch_shapes=[
            pltpu.VMEM(((rows + 2) * wide, 3 * width), BF16),
            pltpu.VMEM((2, total + 2, width), F32),
            pltpu.VMEM((rows, cols, width), BF16),
            pltpu.SemaphoreType.DMA,
        ],
        input_output_aliases={5: 0} if more else {},
        compiler_params=params(20),
        cost_estimate=conv_cost(rows, cols, width),
    )(taps, field, ends, sides, weights, *more)


def patch(window, ends, sides):
    _, cols, width = ends.shape
    wide = padded_width(cols)
    total = sides.shape[1] - 2

    def body(old, ends, sides, window, side_rows):
        side_rows[...] = sides[...].astype(F32)
        for slot, k in ((0, 0), (total + 1, 1)):
            parts = shifted(ends[k], side_rows[0, slot : slot + 1], side_rows[1, slot : slot + 1], wide)
            for tap, part in enumerate(parts):
                window[slot * wide : (slot + 1) * wide, tap * width : (tap + 1) * width] = part
        place = lax.broadcasted_iota(jnp.int32, (16, width), 0)
        last = (cols - 1) // 16 * 16

        @pl.loop(1, total + 1)
        def _(slot):
            for k, (offset, at) in enumerate(((0, 0), (last, cols - 1 - last))):
                where = (pl.ds(pl.multiple_of(slot * wide + offset, 16), 16), slice(2 * k * width, (2 * k + 1) * width))
                value = window[where].astype(F32)
                window[where] = jnp.where(place == at, side_rows[k, pl.ds(slot, 1)], value).astype(BF16)

    return pl.pallas_call(
        body,
        out_shape=jax.ShapeDtypeStruct(window.shape, BF16),
        in_specs=[VMEM] * 3,
        out_specs=VMEM,
        scratch_shapes=[pltpu.VMEM((2, total + 2, width), F32)],
        input_output_aliases={0: 0},
        compiler_params=params(8),
        cost_estimate=pl.CostEstimate(flops=0, bytes_accessed=256 * total * width, transcendentals=0),
    )(window, ends, sides)


def forward(window, weights, shape, first, rows, out=None):
    total, cols, width = shape
    wide = padded_width(cols)
    more = [] if out is None else [out]

    def body(window, weights, *rest):
        out, result, sem = rest[-3:]
        view = window.at[first * wide : (first + rows + 2) * wide]
        conv_rows(None, view, weights, result, out, sem, cols, first, rows, total)

    return pl.pallas_call(
        body,
        out_shape=jax.ShapeDtypeStruct(shape, BF16),
        in_specs=[VMEM, VMEM] + [HBM] * len(more),
        out_specs=HBM,
        scratch_shapes=[pltpu.VMEM((rows, cols, width), BF16), pltpu.SemaphoreType.DMA],
        input_output_aliases={2: 0} if more else {},
        compiler_params=params(8),
        cost_estimate=conv_cost(rows, cols, width),
    )(window, weights, *more)


def turn_group(wide):
    return 128 // math.gcd(128, wide)


def row_messages(rows, inputs, cotangent):
    _, cols, width = inputs.shape

    def body(rows, inputs, cotangent, near, far, sem):
        copies = [
            pltpu.make_async_copy(field.at[rows[k]], out.at[j], sem.at[2 * k + j])
            for k, out in enumerate((near, far))
            for j, field in enumerate((inputs, cotangent))
        ]
        for copy in copies:
            copy.start()
        for copy in copies:
            copy.wait()

    shape = jax.ShapeDtypeStruct((2, cols, width), BF16)
    return pl.pallas_call(
        body,
        out_shape=(shape, shape),
        in_specs=[SMEM, HBM, HBM],
        out_specs=(VMEM, VMEM),
        scratch_shapes=[pltpu.SemaphoreType.DMA((4,))],
        compiler_params=params(8),
    )(rows, inputs, cotangent)


def fetch_chunk(total):
    return max(n for n in range(1, 33) if total % n == 0)


def begin_kernel(field_hbm, cot_hbm, columns, window, turned, taps, cot, field, column_rows, sems):
    total, cols, width = field.shape
    wide = padded_width(cols)
    part = fetch_chunk(total)
    copies = [
        pltpu.make_async_copy(source.at[pl.ds(at, part)], target.at[pl.ds(at, part)], sems.at[at // part, j])
        for at in range(0, total, part)
        for j, (source, target) in enumerate(((cot_hbm, cot), (field_hbm, field)))
    ]
    for copy in copies:
        copy.start()
    empty = jnp.zeros((1, width), F32)
    blank = jnp.zeros((wide - cols, width), F32)
    group = turn_group(wide)
    span = group * wide
    for k in range(3):
        window[0:wide, k * width : (k + 1) * width] = jnp.zeros((wide, width), BF16)
        window[(total + 1) * wide : (total + 2) * wide, k * width : (k + 1) * width] = jnp.zeros((wide, width), BF16)

    for at in range(0, total, part):
        copies[2 * (at // part)].wait()
        copies[2 * (at // part) + 1].wait()

        @pl.loop(at, at + part)
        def _(r):
            row, other = field[r], cot[r]
            start = pl.multiple_of((r + 1) * wide, 16)
            for tap, piece in enumerate(shifted(row, empty, empty, wide)):
                window[pl.ds(start, wide), tap * width : (tap + 1) * width] = piece
            for k, value in enumerate((row, other)):
                value = value.astype(F32)
                column_rows[2 * k, pl.ds(r, 1)] = value[0:1]
                column_rows[2 * k + 1, pl.ds(r, 1)] = value[cols - 1 : cols]

    columns[...] = column_rows[...].astype(BF16)

    def chunk(start, count):
        return [part for j in range(count) for part in (cot[start + j].astype(F32), blank)]

    @pl.loop(0, total // group)
    def _(i):
        value = jnp.concatenate(chunk(i * group, group), 0)
        turned[:, pl.ds(pl.multiple_of(i * span, 128), span)] = value.T.astype(BF16)

    rest = total % group
    if rest:
        start = total - rest
        value = jnp.concatenate(chunk(start, rest) + [jnp.zeros((span - rest * wide, width), F32)], 0)
        turned[:, start * wide : start * wide + span] = value.T.astype(BF16)
    tap_row(turned, window, taps, total * wide, wide, 0)


def tap_row(turned, window, taps, cells, start, slot):
    width = taps.shape[-1]
    value = jnp.dot(turned[:, :cells], window[start : start + cells, :], preferred_element_type=F32)
    for b in range(3):
        taps[slot + b] = value[:, b * width : (b + 1) * width].T


def begin(field, cot):
    total, cols, width = field.shape
    wide = padded_width(cols)
    group = turn_group(wide)
    return pl.pallas_call(
        begin_kernel,
        out_shape=(
            jax.ShapeDtypeStruct((4, total, width), BF16),
            jax.ShapeDtypeStruct(((total + 2) * wide, 3 * width), BF16),
            jax.ShapeDtypeStruct((width, -(-total // group) * group * wide), BF16),
            jax.ShapeDtypeStruct((3, width, width), F32),
            jax.ShapeDtypeStruct(cot.shape, BF16),
        ),
        in_specs=[HBM, HBM],
        out_specs=(VMEM,) * 5,
        scratch_shapes=[
            pltpu.VMEM(field.shape, BF16),
            pltpu.VMEM((4, total, width), F32),
            pltpu.SemaphoreType.DMA((total // fetch_chunk(total), 2)),
        ],
        compiler_params=params(20),
        cost_estimate=pl.CostEstimate(
            flops=8 * total * wide * width * width, bytes_accessed=4 * total * wide * width, transcendentals=0
        ),
    )(field, cot)


def flip(kernel):
    width = kernel.shape[-1]

    def body(kernel, out):
        for tap in range(9):
            a, b = divmod(tap, 3)
            out[a, b * width : (b + 1) * width] = kernel[2 - a, 2 - b].astype(F32).T.astype(BF16)

    return pl.pallas_call(
        body,
        out_shape=jax.ShapeDtypeStruct((3, 3 * width, width), BF16),
        in_specs=[VMEM],
        out_specs=VMEM,
        compiler_params=params(8),
        cost_estimate=pl.CostEstimate(flops=0, bytes_accessed=36 * width * width, transcendentals=0),
    )(kernel)


def outer_taps(window, turned, total, wide):
    width = turned.shape[0]

    def body(window, turned, taps):
        tap_row(turned, window, taps, total * wide, 0, 0)
        tap_row(turned, window, taps, total * wide, 2 * wide, 3)

    return pl.pallas_call(
        body,
        out_shape=jax.ShapeDtypeStruct((6, width, width), F32),
        in_specs=[VMEM, VMEM],
        out_specs=VMEM,
        compiler_params=params(8),
        cost_estimate=pl.CostEstimate(
            flops=12 * total * wide * width * width, bytes_accessed=4 * total * wide * width, transcendentals=0
        ),
    )(window, turned)


def edge_kernel(half, middle, outer, ends, sides, rows, columns, send, keep, side_rows):
    _, cols, width = ends.shape
    wide = padded_width(cols)
    total = columns.shape[1]
    tall = -(-total // 16) * 16
    side_rows[...] = sides[...].astype(F32)
    empty = jnp.zeros((1, width), F32)
    end_parts = [shifted(ends[k], empty, empty, wide) for k in range(2)]
    blank = jnp.zeros((wide - cols, width), F32)
    row_parts = [jnp.concatenate([rows[k].astype(F32), blank], 0).astype(BF16) for k in range(2)]
    low = jnp.zeros((tall - total, width), F32)
    column_parts = [jnp.concatenate([columns[k].astype(F32), low], 0).astype(BF16) for k in range(2)]
    size = 9 * width // 2
    for tap in range(9):
        a, b = divmod(tap, 3)
        left, right = [], []
        if b != 1:
            side = b // 2
            left.append(jnp.concatenate([side_rows[side, a : a + total], low], 0).astype(BF16))
            right.append(column_parts[side])
        if a != 1:
            left.append(end_parts[a // 2][b])
            right.append(row_parts[a // 2])
        value = middle[b] if a == 1 else outer[3 * (a // 2) + b]
        if left:
            value = value + lax.dot_general(
                jnp.concatenate(left, 0),
                jnp.concatenate(right, 0),
                (((0,), (0,)), ((), ())),
                preferred_element_type=F32,
            )
        for part in range(2):
            start = tap * width + part * width // 2
            which, start = divmod(start, size)
            piece = value[part * width // 2 : (part + 1) * width // 2]
            at = slice(start, start + width // 2)

            @pl.when(half[0] == which)
            def _():
                keep[at] = piece

            @pl.when(half[0] != which)
            def _():
                send[at] = piece


def with_edges(half, middle, outer, ends, sides, rows, columns):
    _, _, width = ends.shape
    total = columns.shape[1]
    shape = jax.ShapeDtypeStruct((9 * width // 2, width), F32)
    return pl.pallas_call(
        edge_kernel,
        out_shape=(shape, shape),
        in_specs=[SMEM] + [VMEM] * 6,
        out_specs=(VMEM, VMEM),
        scratch_shapes=[pltpu.VMEM((2, total + 2, width), F32)],
        compiler_params=params(12),
        cost_estimate=pl.CostEstimate(
            flops=16 * 144 * width * width, bytes_accessed=72 * width * width, transcendentals=0
        ),
    )(half, middle, outer, ends, sides, rows, columns)


def add_blocks(places, terms, blocks, scale=None):
    rows, width = terms[0].shape
    size = rows // blocks
    count = places.shape[0]

    def body(where, *refs):
        sources, outs = refs[: len(terms)], refs[len(terms) :]
        for k in range(count):
            at = pl.ds(pl.multiple_of(where[k] * size, 8), size)
            value = sources[0][at]
            for source in sources[1:]:
                value = value + source[at]
            outs[k][...] = value if scale is None else value * scale

    shape = jax.ShapeDtypeStruct((size, width), F32)
    return pl.pallas_call(
        body,
        out_shape=(shape,) * count,
        in_specs=[SMEM] + [VMEM] * len(terms),
        out_specs=(VMEM,) * count,
        compiler_params=params(8),
        cost_estimate=pl.CostEstimate(
            flops=rows * width, bytes_accessed=4 * rows * width * (len(terms) + 1), transcendentals=0
        ),
    )(places, *terms)


def last_sum(terms, scale):
    rows, width = terms[0].shape

    def body(first, second, out):
        value = (first[...] + second[...]) * scale
        top = jnp.max(jnp.max(jnp.abs(value), axis=1, keepdims=True), axis=0, keepdims=True)
        exponent = jnp.ceil(jnp.log2(jnp.maximum(top, 1e-30)))
        out[:rows] = value * jnp.exp2(-exponent)
        out[rows:] = jnp.broadcast_to(exponent, (16, width))

    return pl.pallas_call(
        body,
        out_shape=jax.ShapeDtypeStruct((rows + 16, width), F32),
        in_specs=[VMEM] * 2,
        out_specs=VMEM,
        compiler_params=params(8),
        cost_estimate=pl.CostEstimate(flops=8 * rows * width, bytes_accessed=12 * rows * width, transcendentals=0),
    )(*terms)


def decode(coded):
    return coded[..., :-16, :].astype(F32) * jnp.exp2(coded[..., -1:, :].astype(F32))


def finish(places, own, other):
    blocks, size, width = own.shape

    def body(where, own, other, out, sem):
        for k in range(2 * blocks):
            source = own if k < blocks else other
            at = pl.multiple_of(where[k] * size, 8)
            pltpu.make_async_copy(source.at[k % blocks], out.at[pl.ds(at, size)], sem).start()
        pltpu.make_async_copy(out, out, sem).wait()

    out = pl.pallas_call(
        body,
        out_shape=jax.ShapeDtypeStruct((2 * blocks * size, width), F32),
        in_specs=[SMEM, VMEM, VMEM],
        out_specs=HBM,
        scratch_shapes=[pltpu.SemaphoreType.DMA],
        compiler_params=params(8),
    )(places, own, other)
    return out.reshape(3, 3, width, width)


def swap(value, axis, mask):
    count = lax.axis_size(axis)
    return lax.ppermute(value, axis, [(i, i ^ mask) for i in range(count)])


def swap_next(value, axis):
    count = lax.axis_size(axis)
    return lax.ppermute(value, axis, [(i, (i + (1 if i % 2 else -1)) % count) for i in range(count)])


def swap_rows(value):
    bands, sectors = lax.axis_size("lat"), lax.axis_size("lon")
    pairs = []
    for band in range(bands):
        for sector in range(sectors):
            if band == 0 or band == bands - 1:
                other = (band, (sector + sectors // 2) % sectors)
            else:
                other = (band + (1 if band % 2 else -1), sector)
            pairs.append((band * sectors + sector, other[0] * sectors + other[1]))
    return lax.ppermute(value, ("lat", "lon"), pairs)


def local(inputs, kernel, cotangent):
    rows, cols, width = inputs.shape
    bands, sectors = lax.axis_size("lat"), lax.axis_size("lon")
    band, sector = lax.axis_index("lat"), lax.axis_index("lon")

    def vector(*values):
        return jnp.stack([jnp.asarray(v, jnp.int32) for v in values])

    mine, place = sector & 1, (sector >> 1) & 1
    odd = band & 1
    facts = dict(
        even_band=odd == 0,
        even_sector=mine == 0,
        half=vector(mine),
        rows=vector((1 - odd) * (rows - 1), odd * (rows - 1)),
        lat=vector(*[band ^ m for m in range(bands)]),
        lon=vector(place, 1 - place),
        poles=vector(jnp.where(band == 0, 2, 0), jnp.where(band == bands - 1, 0, 2)),
        last=vector(
            *[
                (h * bands + (band ^ m)) * 2 + p
                for h in (mine, 1 - mine)
                for m in range(bands)
                for p in (place, 1 - place)
            ]
        ),
    )
    inputs, kernel, cotangent, facts = lax.optimization_barrier((inputs, kernel, cotangent, facts))
    even_band, even_sector, half = facts["even_band"], facts["even_sector"], facts["half"]

    near, far = row_messages(facts["rows"], inputs, cotangent)
    near = swap(near, "lat", 1)
    far = swap_rows(far)
    columns, window, turned, middle, cot = begin(inputs, cotangent)
    ends = jnp.stack([jnp.where(even_band, far, near), jnp.where(even_band, near, far)], 1)

    def side(place):
        column = 0 if place == 0 else cols - 1
        return jnp.stack(
            [
                jnp.concatenate([ends[k, :1, column], columns[2 * k + place], ends[k, 1:, column]], 0)
                for k in range(2)
            ]
        )

    first, last = side(0), side(1)
    near = swap(jnp.where(even_sector, last, first), "lon", 1)
    far = swap_next(jnp.where(even_sector, first, last), "lon")
    outer = outer_taps(window, turned, rows, padded_width(cols))
    sides = jnp.stack([jnp.where(even_sector, far, near), jnp.where(even_sector, near, far)], 1)

    edge_rows = jnp.stack([cotangent[0], cotangent[-1]])
    send, keep = with_edges(half, middle, outer, ends[0], sides[0], edge_rows, columns[2:])

    weights = kernel.reshape(3, 3 * width, width)
    flipped = flip(kernel)
    window = patch(window, ends[0], sides[0])
    outputs = input_grad = None
    for start, count in pieces(rows, FORWARD):
        outputs = forward(window, weights, inputs.shape, start, count, outputs)
    for start, count in pieces(rows, BACKWARD):
        input_grad = backward(facts["poles"], cot, ends[1], sides[1], flipped, start, count, input_grad)

    got = swap(send, "lon", 1)
    parts = add_blocks(facts["lat"], [keep, got], bands)
    got = []
    for m in range(1, bands):
        got.append(swap(parts[m], "lat", m))
    keep, send = add_blocks(facts["lon"], [parts[0], *got], 2)
    got = swap(send, "lon", 2)
    factor = 1.0 / math.sqrt(rows * cols * bands * sectors)
    mask = 4
    terms = [keep, got]
    while mask < sectors:
        value = terms[0] + terms[1]
        terms = [value, swap(value, "lon", mask)]
        mask *= 2

    coded = last_sum(terms, factor).astype(HALF)
    got = swap(coded, "lon", 2)
    coded = jnp.stack([coded, got])
    got = []
    for m in range(1, bands):
        got.append(swap(coded, "lat", m))
    coded = jnp.stack([coded, *got])
    got = swap(coded, "lon", 1)
    own, other = (decode(c).reshape(2 * bands, -1, width) for c in (coded, got))
    kernel_grad = finish(facts["last"], own, other)
    return (outputs, input_grad, kernel_grad)


FORWARD = (0, 90)
BACKWARD = (0, 30, 60, 75, 90)


def pieces(rows, cuts):
    if cuts[-1] != rows:
        cuts = (0, rows)
    return [(low, high - low) for low, high in zip(cuts, cuts[1:])]


def solution(mesh):
    in_specs = (P("lat", "lon", None), P(), P("lat", "lon", None))
    out_specs = (P("lat", "lon", None), P("lat", "lon", None), P())
    return jax.shard_map(local, mesh=mesh, in_specs=in_specs, out_specs=out_specs, check_vma=False)
```

```python
import math

import jax
import jax.numpy as jnp
from jax import lax
from jax.experimental import pallas as pl
from jax.experimental.pallas import tpu as pltpu
from jax.sharding import PartitionSpec as P


F32 = jnp.float32
BF16 = jnp.bfloat16
HALF = jnp.float16
VMEM = pl.BlockSpec(memory_space=pltpu.VMEM)
SMEM = pl.BlockSpec(memory_space=pltpu.SMEM)
HBM = pl.BlockSpec(memory_space=pltpu.HBM)


def padded_width(cols):
    return -(-(cols + 3) // 16) * 16


def in_hbm(value):
    return pltpu.with_memory_space_constraint(value, pltpu.HBM)


def params(mib):
    return pltpu.CompilerParams(vmem_limit_bytes=mib << 20)


def shifted(row, left, right, wide):
    cols, width = row.shape
    middle = jnp.zeros((wide - cols - 2, width), F32)
    base = jnp.concatenate([row.astype(F32), right, middle, left], 0)
    return (
        pltpu.roll(base, 1, 0).astype(BF16),
        base.astype(BF16),
        pltpu.roll(base, wide - 1, 0).astype(BF16),
    )


def fill_window(field, ends, sides, side_rows, window, first, rows):
    total, cols, width = field.shape
    wide = padded_width(cols)
    side_rows[...] = sides[...].astype(F32)

    def put(slot, row, at):
        parts = shifted(row, side_rows[0, pl.ds(at, 1)], side_rows[1, pl.ds(at, 1)], wide)
        start = slot * wide if isinstance(slot, int) else pl.multiple_of(slot * wide, 16)
        for tap, part in enumerate(parts):
            window[pl.ds(start, wide), tap * width : (tap + 1) * width] = part

    low = 0
    if first == 0:
        put(0, ends[0], 0)
        low = 1
    high = rows + 2
    if first + rows == total:
        put(rows + 1, ends[1], total + 1)
        high = rows + 1

    @pl.loop(low, high)
    def _(slot):
        put(slot, field[first + slot - 1], first + slot)


def block_rows(rows):
    return max(n for n in range(1, 6) if rows % n == 0)


def conv_rows(taps, window, weights, result, cols, first, rows, total):
    width = weights.shape[-1]
    wide = padded_width(cols)
    step = block_rows(rows)

    def term(slot, count, which):
        at = slot * wide if isinstance(slot, int) else pl.multiple_of(slot * wide, 16)
        return jnp.dot(window[pl.ds(at, count * wide), :], weights[which], preferred_element_type=F32)

    def block(i, top=0, bottom=2):
        start = i * step
        if isinstance(top, int):
            value = term(start, step, 0)
        else:
            value = jnp.concatenate([term(start, 1, top), term(start + 1, step - 1, 0)], 0)
        value = value + term(start + 1, step, 1)
        if isinstance(bottom, int):
            value = value + term(start + 2, step, 2)
        else:
            value = value + jnp.concatenate(
                [term(start + 2, step - 1, 2), term(start + step + 1, 1, bottom)], 0
            )
        result[pl.ds(start, step)] = value.reshape(step, wide, width)[:, :cols].astype(BF16)

    count = rows // step
    poles = taps is not None and step > 1
    low = int(first == 0 and poles)
    high = count - int(first + rows == total and poles)
    group = 3
    trips = (high - low) // group

    @pl.loop(0, trips)
    def _(j):
        for u in range(group):
            block(low + j * group + u)

    for i in range(low + trips * group, high):
        block(i)
    if low:
        block(0, top=taps[0])
    if high < count:
        block(count - 1, bottom=taps[1])


def conv_cost(rows, cols, width):
    wide = padded_width(cols)
    return pl.CostEstimate(
        flops=18 * rows * wide * width * width, bytes_accessed=4 * rows * wide * width, transcendentals=0
    )


def prepare(field, ends, sides):
    total, cols, width = field.shape
    wide = padded_width(cols)

    def body(field, ends, sides, window, side_rows):
        fill_window(field, ends, sides, side_rows, window, 0, total)

    return pl.pallas_call(
        body,
        out_shape=jax.ShapeDtypeStruct(((total + 2) * wide, 3 * width), BF16),
        in_specs=[VMEM] * 3,
        out_specs=VMEM,
        scratch_shapes=[pltpu.VMEM((2, total + 2, width), F32)],
        compiler_params=params(8),
        cost_estimate=pl.CostEstimate(flops=0, bytes_accessed=8 * total * wide * width, transcendentals=0),
    )(field, ends, sides)


def patch(window, ends, sides):
    _, cols, width = ends.shape
    wide = padded_width(cols)
    total = sides.shape[1] - 2

    def body(old, ends, sides, window, side_rows):
        side_rows[...] = sides[...].astype(F32)
        for slot, k in ((0, 0), (total + 1, 1)):
            parts = shifted(ends[k], side_rows[0, slot : slot + 1], side_rows[1, slot : slot + 1], wide)
            for tap, part in enumerate(parts):
                window[slot * wide : (slot + 1) * wide, tap * width : (tap + 1) * width] = part
        place = lax.broadcasted_iota(jnp.int32, (16, width), 0)
        last = (cols - 1) // 16 * 16

        @pl.loop(1, total + 1)
        def _(slot):
            for k, (offset, at) in enumerate(((0, 0), (last, cols - 1 - last))):
                where = (pl.ds(pl.multiple_of(slot * wide + offset, 16), 16), slice(2 * k * width, (2 * k + 1) * width))
                value = window[where].astype(F32)
                window[where] = jnp.where(place == at, side_rows[k, pl.ds(slot, 1)], value).astype(BF16)

    return pl.pallas_call(
        body,
        out_shape=jax.ShapeDtypeStruct(window.shape, BF16),
        in_specs=[VMEM] * 3,
        out_specs=VMEM,
        scratch_shapes=[pltpu.VMEM((2, total + 2, width), F32)],
        input_output_aliases={0: 0},
        compiler_params=params(8),
        cost_estimate=pl.CostEstimate(flops=0, bytes_accessed=256 * total * width, transcendentals=0),
    )(window, ends, sides)


class Flush:
    def __init__(self):
        self.piece = self.first = self.name = None
        self.outputs = {}

    def operands(self):
        if self.piece is None:
            return []
        known = self.outputs.get(self.name)
        return [self.piece] if known is None else [self.piece, known]

    def specs(self):
        return [VMEM, HBM][: len(self.operands())]

    def shapes(self, shape):
        return [] if self.piece is None else [jax.ShapeDtypeStruct(shape, BF16)]

    def aliases(self, operand, output):
        return {operand + 1: output} if len(self.operands()) == 2 else {}

    def scratch(self):
        return [] if self.piece is None else [pltpu.SemaphoreType.DMA]

    def copy(self, piece, out, sem):
        return pltpu.make_async_copy(piece, out.at[pl.ds(self.first, self.piece.shape[0])], sem)


def conv(taps, window, weights, shape, first, rows, name, flush):
    total, cols, width = shape
    wide = padded_width(cols)
    flags = [] if taps is None else [taps]
    more = flush.operands()
    inputs = len(flags) + 2

    def body(*refs):
        taps = refs[0] if flags else None
        window, weights = refs[len(flags) : inputs]
        result = refs[inputs + len(more)]
        copy = None
        if more:
            copy = flush.copy(refs[inputs], refs[-2], refs[-1])
            copy.start()
        view = window.at[first * wide : (first + rows + 2) * wide]
        conv_rows(taps, view, weights, result, cols, first, rows, total)
        if copy is not None:
            copy.wait()

    results = pl.pallas_call(
        body,
        out_shape=[jax.ShapeDtypeStruct((rows, cols, width), BF16)] + flush.shapes(shape),
        in_specs=[SMEM] * len(flags) + [VMEM] * 2 + flush.specs(),
        out_specs=[VMEM] + [HBM] * bool(more),
        scratch_shapes=flush.scratch(),
        input_output_aliases=flush.aliases(inputs, 1),
        compiler_params=params(8),
        cost_estimate=conv_cost(rows, cols, width),
    )(*flags, window, weights, *more)
    if more:
        flush.outputs[flush.name] = results[1]
    flush.piece, flush.first, flush.name = results[0], first, name


def turn_group(wide):
    return 128 // math.gcd(128, wide)


def fetch_chunk(total):
    return max(n for n in range(1, 19) if total % n == 0)


def begin_kernel(field_hbm, cot_hbm, columns, window, turned, taps, cot, field, column_rows, sems):
    total, cols, width = field.shape
    wide = padded_width(cols)
    part = fetch_chunk(total)
    copies = [
        pltpu.make_async_copy(source.at[pl.ds(at, part)], target.at[pl.ds(at, part)], sems.at[at // part, j])
        for at in range(0, total, part)
        for j, (source, target) in enumerate(((cot_hbm, cot), (field_hbm, field)))
    ]
    for copy in copies:
        copy.start()
    empty = jnp.zeros((1, width), F32)
    blank = jnp.zeros((wide - cols, width), F32)
    group = turn_group(wide)
    span = group * wide
    for k in range(3):
        window[0:wide, k * width : (k + 1) * width] = jnp.zeros((wide, width), BF16)
        window[(total + 1) * wide : (total + 2) * wide, k * width : (k + 1) * width] = jnp.zeros((wide, width), BF16)

    for at in range(0, total, part):
        copies[2 * (at // part)].wait()
        copies[2 * (at // part) + 1].wait()

        @pl.loop(at, at + part)
        def _(r):
            row, other = field[r], cot[r]
            start = pl.multiple_of((r + 1) * wide, 16)
            for tap, piece in enumerate(shifted(row, empty, empty, wide)):
                window[pl.ds(start, wide), tap * width : (tap + 1) * width] = piece
            for k, value in enumerate((row, other)):
                value = value.astype(F32)
                column_rows[2 * k, pl.ds(r, 1)] = value[0:1]
                column_rows[2 * k + 1, pl.ds(r, 1)] = value[cols - 1 : cols]

    columns[...] = column_rows[...].astype(BF16)

    def chunk(start, count):
        return [part for j in range(count) for part in (cot[start + j].astype(F32), blank)]

    @pl.loop(0, total // group)
    def _(i):
        value = jnp.concatenate(chunk(i * group, group), 0)
        turned[:, pl.ds(pl.multiple_of(i * span, 128), span)] = value.T.astype(BF16)

    rest = total % group
    if rest:
        start = total - rest
        value = jnp.concatenate(chunk(start, rest) + [jnp.zeros((span - rest * wide, width), F32)], 0)
        turned[:, start * wide : start * wide + span] = value.T.astype(BF16)
    tap_row(turned, window, taps, total * wide, wide, 0)


def tap_row(turned, window, taps, cells, start, slot):
    width = taps.shape[-1]
    value = jnp.dot(turned[:, :cells], window[start : start + cells, :], preferred_element_type=F32)
    for b in range(3):
        taps[slot + b] = value[:, b * width : (b + 1) * width].T


def begin(field, cot):
    total, cols, width = field.shape
    wide = padded_width(cols)
    group = turn_group(wide)
    return pl.pallas_call(
        begin_kernel,
        out_shape=(
            jax.ShapeDtypeStruct((4, total, width), BF16),
            jax.ShapeDtypeStruct(((total + 2) * wide, 3 * width), BF16),
            jax.ShapeDtypeStruct((width, -(-total // group) * group * wide), BF16),
            jax.ShapeDtypeStruct((3, width, width), F32),
            jax.ShapeDtypeStruct(cot.shape, BF16),
        ),
        in_specs=[HBM, HBM],
        out_specs=(VMEM,) * 5,
        scratch_shapes=[
            pltpu.VMEM(field.shape, BF16),
            pltpu.VMEM((4, total, width), F32),
            pltpu.SemaphoreType.DMA((total // fetch_chunk(total), 2)),
        ],
        compiler_params=params(12),
        cost_estimate=pl.CostEstimate(
            flops=8 * total * wide * width * width, bytes_accessed=4 * total * wide * width, transcendentals=0
        ),
    )(field, cot)


def flip(kernel):
    width = kernel.shape[-1]

    def body(kernel, out):
        for tap in range(9):
            a, b = divmod(tap, 3)
            out[a, b * width : (b + 1) * width] = kernel[2 - a, 2 - b].astype(F32).T.astype(BF16)

    return pl.pallas_call(
        body,
        out_shape=jax.ShapeDtypeStruct((3, 3 * width, width), BF16),
        in_specs=[VMEM],
        out_specs=VMEM,
        compiler_params=params(8),
        cost_estimate=pl.CostEstimate(flops=0, bytes_accessed=36 * width * width, transcendentals=0),
    )(kernel)


def outer_taps(window, turned, total, wide):
    width = turned.shape[0]

    def body(window, turned, taps):
        tap_row(turned, window, taps, total * wide, 0, 0)
        tap_row(turned, window, taps, total * wide, 2 * wide, 3)

    return pl.pallas_call(
        body,
        out_shape=jax.ShapeDtypeStruct((6, width, width), F32),
        in_specs=[VMEM, VMEM],
        out_specs=VMEM,
        compiler_params=params(8),
        cost_estimate=pl.CostEstimate(
            flops=12 * total * wide * width * width, bytes_accessed=4 * total * wide * width, transcendentals=0
        ),
    )(window, turned)


def edge_kernel(half, middle, outer, ends, sides, rows, columns, send, every, side_rows):
    _, cols, width = ends.shape
    wide = padded_width(cols)
    total = columns.shape[1]
    tall = -(-total // 16) * 16
    side_rows[...] = sides[...].astype(F32)
    empty = jnp.zeros((1, width), F32)
    end_parts = [shifted(ends[k], empty, empty, wide) for k in range(2)]
    blank = jnp.zeros((wide - cols, width), F32)
    row_parts = [jnp.concatenate([rows[k].astype(F32), blank], 0).astype(BF16) for k in range(2)]
    low = jnp.zeros((tall - total, width), F32)
    column_parts = [jnp.concatenate([columns[k].astype(F32), low], 0).astype(BF16) for k in range(2)]
    size = 9 * width // 2
    for tap in range(9):
        a, b = divmod(tap, 3)
        left, right = [], []
        if b != 1:
            side = b // 2
            left.append(jnp.concatenate([side_rows[side, a : a + total], low], 0).astype(BF16))
            right.append(column_parts[side])
        if a != 1:
            left.append(end_parts[a // 2][b])
            right.append(row_parts[a // 2])
        value = middle[b] if a == 1 else outer[3 * (a // 2) + b]
        if left:
            value = value + lax.dot_general(
                jnp.concatenate(left, 0),
                jnp.concatenate(right, 0),
                (((0,), (0,)), ((), ())),
                preferred_element_type=F32,
            )
        every[tap * width : (tap + 1) * width] = value
    send[...] = every[pl.ds(pl.multiple_of((1 - half[0]) * size, 8), size)]


def with_edges(half, middle, outer, ends, sides, rows, columns):
    _, _, width = ends.shape
    total = columns.shape[1]
    return pl.pallas_call(
        edge_kernel,
        out_shape=(
            jax.ShapeDtypeStruct((9 * width // 2, width), F32),
            jax.ShapeDtypeStruct((9 * width, width), F32),
        ),
        in_specs=[SMEM] + [VMEM] * 6,
        out_specs=(VMEM, VMEM),
        scratch_shapes=[pltpu.VMEM((2, total + 2, width), F32)],
        compiler_params=params(12),
        cost_estimate=pl.CostEstimate(
            flops=16 * 144 * width * width, bytes_accessed=72 * width * width, transcendentals=0
        ),
    )(half, middle, outer, ends, sides, rows, columns)


def add_blocks(places, terms, sizes):
    width = terms[0].shape[1]
    count = len(sizes)

    def body(where, *refs):
        sources, outs = refs[: len(terms)], refs[len(terms) :]
        for k, size in enumerate(sizes):
            value = None
            for t, source in enumerate(sources):
                part = source[pl.ds(pl.multiple_of(where[t * count + k], 8), size)]
                value = part if value is None else value + part
            outs[k][...] = value

    return pl.pallas_call(
        body,
        out_shape=tuple(jax.ShapeDtypeStruct((size, width), F32) for size in sizes),
        in_specs=[SMEM] + [VMEM] * len(terms),
        out_specs=(VMEM,) * count,
        compiler_params=params(8),
        cost_estimate=pl.CostEstimate(
            flops=sum(sizes) * width, bytes_accessed=4 * sum(sizes) * width * (len(terms) + 1), transcendentals=0
        ),
    )(places, *terms)


def join_sums(upper, lower):
    above, width = upper[0].shape
    below = lower[0].shape[0]

    def body(*refs):
        out = refs[-1]
        for at, size, sources in ((0, above, refs[: len(upper)]), (above, below, refs[len(upper) : -1])):
            value = sources[0][...]
            for source in sources[1:]:
                value = value + source[...]
            out[at : at + size] = value

    return pl.pallas_call(
        body,
        out_shape=jax.ShapeDtypeStruct((above + below, width), F32),
        in_specs=[VMEM] * (len(upper) + len(lower)),
        out_specs=VMEM,
        compiler_params=params(8),
        cost_estimate=pl.CostEstimate(
            flops=4 * (above + below) * width, bytes_accessed=16 * (above + below) * width, transcendentals=0
        ),
    )(*upper, *lower)


def last_sum(terms, scale):
    rows, width = terms[0].shape

    def body(first, second, out):
        value = (first[...] + second[...]) * scale
        top = jnp.max(jnp.max(jnp.abs(value), axis=1, keepdims=True), axis=0, keepdims=True)
        exponent = jnp.ceil(jnp.log2(jnp.maximum(top, 1e-30)))
        out[:rows] = value * jnp.exp2(-exponent)
        out[rows:] = jnp.broadcast_to(exponent, (8, width))

    return pl.pallas_call(
        body,
        out_shape=jax.ShapeDtypeStruct((rows + 8, width), F32),
        in_specs=[VMEM] * 2,
        out_specs=VMEM,
        compiler_params=params(8),
        cost_estimate=pl.CostEstimate(flops=8 * rows * width, bytes_accessed=12 * rows * width, transcendentals=0),
    )(*terms)


def decode(coded):
    return coded[..., :-8, :].astype(F32) * jnp.exp2(coded[..., -1:, :].astype(F32))


def put_blocks(places, blocks, cuts, total, out=None, flush=None, shape=None):
    count, _, width = blocks.shape
    more = [] if out is None else [out]
    late = [] if flush is None else flush.operands()
    inputs = 2 + len(more)

    def body(where, blocks, *rest):
        refs = rest[len(more) + len(late) :]
        out, sem = refs[0], refs[-1]
        copy = None
        if late:
            copy = flush.copy(rest[len(more)], refs[1], refs[2])
            copy.start()
        for k in range(count):
            start = 0
            for j, size in enumerate(cuts):
                at = pl.multiple_of(where[2 * k + j], 8)
                pltpu.make_async_copy(blocks.at[k, pl.ds(start, size)], out.at[pl.ds(at, size)], sem).start()
                start += size
        pltpu.make_async_copy(blocks, blocks, sem).wait()
        if copy is not None:
            copy.wait()

    results = pl.pallas_call(
        body,
        out_shape=[jax.ShapeDtypeStruct((total, width), F32)] + (flush.shapes(shape) if late else []),
        in_specs=[SMEM, VMEM] + [HBM] * len(more) + (flush.specs() if late else []),
        out_specs=[HBM] * (1 + bool(late)),
        scratch_shapes=(flush.scratch() if late else []) + [pltpu.SemaphoreType.DMA],
        input_output_aliases={**({2: 0} if more else {}), **(flush.aliases(inputs, 1) if late else {})},
        compiler_params=params(8),
    )(places, blocks, *more, *late)
    if late:
        flush.outputs[flush.name] = results[1]
    return results[0]


def swap(value, axis, mask):
    count = lax.axis_size(axis)
    return lax.ppermute(value, axis, [(i, i ^ mask) for i in range(count)])


def swap_next(value, axis):
    count = lax.axis_size(axis)
    return lax.ppermute(value, axis, [(i, (i + (1 if i % 2 else -1)) % count) for i in range(count)])


def swap_rows(value):
    bands, sectors = lax.axis_size("lat"), lax.axis_size("lon")
    pairs = []
    for band in range(bands):
        for sector in range(sectors):
            if band == 0 or band == bands - 1:
                other = (band, (sector + sectors // 2) % sectors)
            else:
                other = (band + (1 if band % 2 else -1), sector)
            pairs.append((band * sectors + sector, other[0] * sectors + other[1]))
    return lax.ppermute(value, ("lat", "lon"), pairs)


def local(inputs, kernel, cotangent):
    rows, cols, width = inputs.shape
    bands, sectors = lax.axis_size("lat"), lax.axis_size("lon")
    band, sector = lax.axis_index("lat"), lax.axis_index("lon")

    def vector(*values):
        return jnp.stack([jnp.asarray(v, jnp.int32) for v in values])

    mine, place = sector & 1, (sector >> 1) & 1
    odd = band & 1
    half_rows = 9 * width // 2
    unit = 16 * bands
    upper = (half_rows // unit + 1) // 2 * unit
    lower = half_rows - upper
    upper_part, lower_part = upper // bands, lower // 2
    upper_end, lower_end = upper_part // 2, lower_part // bands
    first_sizes = [upper_part] * bands + [lower_part] * 2
    first_rows = [(band ^ m) * upper_part for m in range(bands)]
    first_rows += [upper + p * lower_part for p in (place, 1 - place)]

    def homes(h):
        return vector(
            *[
                h * half_rows + row
                for m in range(bands)
                for p in (place, 1 - place)
                for row in (
                    (band ^ m) * upper_part + p * upper_end,
                    upper + p * lower_part + (band ^ m) * lower_end,
                )
            ]
        )

    facts = dict(
        even_band=odd == 0,
        even_sector=mine == 0,
        half=vector(mine),
        near_row=(1 - odd) * (rows - 1),
        far_row=odd * (rows - 1),
        first=vector(*[mine * half_rows + row for row in first_rows], *first_rows),
        upper=vector(*[p * upper_end for _ in range(bands) for p in (place, 1 - place)]),
        lower=vector(*[(band ^ m) * lower_end for _ in range(2) for m in range(bands)]),
        poles=vector(jnp.where(band == 0, 2, 0), jnp.where(band == bands - 1, 0, 2)),
        own=homes(mine),
        other=homes(1 - mine),
    )
    inputs, kernel, cotangent, facts = lax.optimization_barrier((inputs, kernel, cotangent, facts))
    even_band, even_sector, half = facts["even_band"], facts["even_sector"], facts["half"]

    near, far = (
        jnp.stack([lax.dynamic_index_in_dim(field, facts[name], 0, False) for field in (inputs, cotangent)])
        for name in ("near_row", "far_row")
    )
    near = swap(near, "lat", 1)
    far = swap_rows(far)
    columns, window, turned, middle, cot = begin(in_hbm(inputs), in_hbm(cotangent))
    ends = jnp.stack([jnp.where(even_band, far, near), jnp.where(even_band, near, far)], 1)

    def side(place):
        column = 0 if place == 0 else cols - 1
        return jnp.stack(
            [
                jnp.concatenate([ends[k, :1, column], columns[2 * k + place], ends[k, 1:, column]], 0)
                for k in range(2)
            ]
        )

    first, last = side(0), side(1)
    near = swap(jnp.where(even_sector, last, first), "lon", 1)
    far = swap_next(jnp.where(even_sector, first, last), "lon")
    outer = outer_taps(window, turned, rows, padded_width(cols))
    sides = jnp.stack([jnp.where(even_sector, far, near), jnp.where(even_sector, near, far)], 1)

    edge_rows = jnp.stack([cotangent[0], cotangent[-1]])
    send, every = with_edges(half, middle, outer, ends[0], sides[0], edge_rows, columns[2:])

    weights = kernel.reshape(3, 3 * width, width)
    flipped = flip(kernel)
    window = patch(window, ends[0], sides[0])
    cot_window = prepare(cot, ends[1], sides[1])
    flush = Flush()
    for name, (start, count) in pieces(rows):
        if name.startswith("forward"):
            conv(None, window, weights, inputs.shape, start, count, "outputs", flush)
        else:
            conv(facts["poles"], cot_window, flipped, inputs.shape, start, count, "input_grad", flush)

    got = swap(send, "lon", 1)
    *parts, low_keep, low_send = add_blocks(facts["first"], [every, got], first_sizes)
    low_got = swap(low_send, "lon", 2)
    got = []
    for m in range(1, bands):
        got.append(swap(parts[m], "lat", m))
    lows = add_blocks(facts["lower"], [low_keep, low_got], [lower_end] * bands)
    keep, send = add_blocks(facts["upper"], [parts[0], *got], [upper_end] * 2)
    low_got = []
    got = swap(send, "lon", 2)
    for m in range(1, bands):
        low_got.append(swap(lows[m], "lat", m))
    value = join_sums([keep, got], [lows[0], *low_got])
    factor = 1.0 / math.sqrt(rows * cols * bands * sectors)
    mask = 4
    while mask < sectors:
        terms = [value, swap(value, "lon", mask)]
        mask *= 2
        if mask < sectors:
            value = terms[0] + terms[1]

    coded = last_sum(terms, factor).astype(HALF)
    got = swap(coded, "lon", 2)
    coded = jnp.stack([coded, got])
    got = []
    for m in range(1, bands):
        got.append(swap(coded, "lat", m))
    coded = jnp.stack([coded, *got])
    got = swap(coded, "lon", 1)
    whole, cuts = 9 * width, (upper_end, lower_end)
    kernel_grad = put_blocks(facts["own"], decode(coded).reshape(2 * bands, -1, width), cuts, whole, None, flush, inputs.shape)
    kernel_grad = put_blocks(facts["other"], decode(got).reshape(2 * bands, -1, width), cuts, whole, kernel_grad)
    return (flush.outputs["outputs"], flush.outputs["input_grad"], kernel_grad.reshape(3, 3, width, width))


FORWARD = (0, 45, 90)
BACKWARD = (0, 45, 60, 90)


def pieces(rows):
    for name, cuts in (("forward", FORWARD), ("backward", BACKWARD)):
        if cuts[-1] != rows:
            cuts = tuple(k * rows // (len(cuts) - 1) for k in range(len(cuts)))
        for k, (low, high) in enumerate(zip(cuts, cuts[1:])):
            yield f"{name}_{k}", (low, high - low)


def solution(mesh):
    in_specs = (P("lat", "lon", None), P(), P("lat", "lon", None))
    out_specs = (P("lat", "lon", None), P("lat", "lon", None), P())
    return jax.shard_map(local, mesh=mesh, in_specs=in_specs, out_specs=out_specs, check_vma=False)
```

```python
import math

import jax
import jax.numpy as jnp
from jax import lax
from jax.experimental import pallas as pl
from jax.experimental.pallas import tpu as pltpu
from jax.sharding import PartitionSpec as P


F32 = jnp.float32
BF16 = jnp.bfloat16
HALF = jnp.float16
VMEM = pl.BlockSpec(memory_space=pltpu.VMEM)
SMEM = pl.BlockSpec(memory_space=pltpu.SMEM)
HBM = pl.BlockSpec(memory_space=pltpu.HBM)


def padded_width(cols):
    return -(-(cols + 3) // 16) * 16


def in_hbm(value):
    return pltpu.with_memory_space_constraint(value, pltpu.HBM)


def params(mib):
    return pltpu.CompilerParams(vmem_limit_bytes=mib << 20)


def shifted(row, left, right, wide):
    cols, width = row.shape
    middle = jnp.zeros((wide - cols - 2, width), F32)
    base = jnp.concatenate([row.astype(F32), right, middle, left], 0)
    return (
        pltpu.roll(base, 1, 0).astype(BF16),
        base.astype(BF16),
        pltpu.roll(base, wide - 1, 0).astype(BF16),
    )


def fill_window(field, ends, sides, side_rows, window, first, rows):
    total, cols, width = field.shape
    wide = padded_width(cols)
    side_rows[...] = sides[...].astype(F32)

    def put(slot, row, at):
        parts = shifted(row, side_rows[0, pl.ds(at, 1)], side_rows[1, pl.ds(at, 1)], wide)
        start = slot * wide if isinstance(slot, int) else pl.multiple_of(slot * wide, 16)
        for tap, part in enumerate(parts):
            window[pl.ds(start, wide), tap * width : (tap + 1) * width] = part

    low = 0
    if first == 0:
        put(0, ends[0], 0)
        low = 1
    high = rows + 2
    if first + rows == total:
        put(rows + 1, ends[1], total + 1)
        high = rows + 1

    @pl.loop(low, high)
    def _(slot):
        put(slot, field[first + slot - 1], first + slot)


def block_rows(rows):
    return max(n for n in range(1, 6) if rows % n == 0)


def conv_rows(taps, window, weights, result, cols, first, rows, total):
    width = weights.shape[-1]
    wide = padded_width(cols)
    step = block_rows(rows)

    def term(slot, count, which):
        at = slot * wide if isinstance(slot, int) else pl.multiple_of(slot * wide, 16)
        return jnp.dot(window[pl.ds(at, count * wide), :], weights[which], preferred_element_type=F32)

    def block(i, top=0, bottom=2):
        start = i * step
        if isinstance(top, int):
            value = term(start, step, 0)
        else:
            value = jnp.concatenate([term(start, 1, top), term(start + 1, step - 1, 0)], 0)
        value = value + term(start + 1, step, 1)
        if isinstance(bottom, int):
            value = value + term(start + 2, step, 2)
        else:
            value = value + jnp.concatenate(
                [term(start + 2, step - 1, 2), term(start + step + 1, 1, bottom)], 0
            )
        result[pl.ds(start, step)] = value.reshape(step, wide, width)[:, :cols].astype(BF16)

    count = rows // step
    poles = taps is not None and step > 1
    low = int(first == 0 and poles)
    high = count - int(first + rows == total and poles)
    group = 3
    trips = (high - low) // group

    @pl.loop(0, trips)
    def _(j):
        for u in range(group):
            block(low + j * group + u)

    for i in range(low + trips * group, high):
        block(i)
    if low:
        block(0, top=taps[0])
    if high < count:
        block(count - 1, bottom=taps[1])


def conv_cost(rows, cols, width):
    wide = padded_width(cols)
    return pl.CostEstimate(
        flops=18 * rows * wide * width * width, bytes_accessed=4 * rows * wide * width, transcendentals=0
    )


def prepare(field, ends, sides):
    total, cols, width = field.shape
    wide = padded_width(cols)

    def body(field, ends, sides, window, side_rows):
        fill_window(field, ends, sides, side_rows, window, 0, total)

    return pl.pallas_call(
        body,
        out_shape=jax.ShapeDtypeStruct(((total + 2) * wide, 3 * width), BF16),
        in_specs=[VMEM] * 3,
        out_specs=VMEM,
        scratch_shapes=[pltpu.VMEM((2, total + 2, width), F32)],
        compiler_params=params(8),
        cost_estimate=pl.CostEstimate(flops=0, bytes_accessed=8 * total * wide * width, transcendentals=0),
    )(field, ends, sides)


def patch(window, ends, sides):
    _, cols, width = ends.shape
    wide = padded_width(cols)
    total = sides.shape[1] - 2

    def body(old, ends, sides, window, side_rows):
        side_rows[...] = sides[...].astype(F32)
        for slot, k in ((0, 0), (total + 1, 1)):
            parts = shifted(ends[k], side_rows[0, slot : slot + 1], side_rows[1, slot : slot + 1], wide)
            for tap, part in enumerate(parts):
                window[slot * wide : (slot + 1) * wide, tap * width : (tap + 1) * width] = part
        place = lax.broadcasted_iota(jnp.int32, (16, width), 0)
        last = (cols - 1) // 16 * 16

        @pl.loop(1, total + 1)
        def _(slot):
            for k, (offset, at) in enumerate(((0, 0), (last, cols - 1 - last))):
                where = (pl.ds(pl.multiple_of(slot * wide + offset, 16), 16), slice(2 * k * width, (2 * k + 1) * width))
                value = window[where].astype(F32)
                window[where] = jnp.where(place == at, side_rows[k, pl.ds(slot, 1)], value).astype(BF16)

    return pl.pallas_call(
        body,
        out_shape=jax.ShapeDtypeStruct(window.shape, BF16),
        in_specs=[VMEM] * 3,
        out_specs=VMEM,
        scratch_shapes=[pltpu.VMEM((2, total + 2, width), F32)],
        input_output_aliases={0: 0},
        compiler_params=params(8),
        cost_estimate=pl.CostEstimate(flops=0, bytes_accessed=256 * total * width, transcendentals=0),
    )(window, ends, sides)


class Flush:
    def __init__(self):
        self.piece = self.first = self.name = None
        self.outputs = {}

    def operands(self):
        if self.piece is None:
            return []
        known = self.outputs.get(self.name)
        return [self.piece] if known is None else [self.piece, known]

    def specs(self):
        return [VMEM, HBM][: len(self.operands())]

    def shapes(self, shape):
        return [] if self.piece is None else [jax.ShapeDtypeStruct(shape, BF16)]

    def aliases(self, operand, output):
        return {operand + 1: output} if len(self.operands()) == 2 else {}

    def scratch(self):
        return [] if self.piece is None else [pltpu.SemaphoreType.DMA]

    def copy(self, piece, out, sem):
        return pltpu.make_async_copy(piece, out.at[pl.ds(self.first, self.piece.shape[0])], sem)


def conv(taps, window, weights, shape, first, rows, name, flush):
    total, cols, width = shape
    wide = padded_width(cols)
    flags = [] if taps is None else [taps]
    more = flush.operands()
    inputs = len(flags) + 2

    def body(*refs):
        taps = refs[0] if flags else None
        window, weights = refs[len(flags) : inputs]
        result = refs[inputs + len(more)]
        copy = None
        if more:
            copy = flush.copy(refs[inputs], refs[-2], refs[-1])
            copy.start()
        view = window.at[first * wide : (first + rows + 2) * wide]
        conv_rows(taps, view, weights, result, cols, first, rows, total)
        if copy is not None:
            copy.wait()

    results = pl.pallas_call(
        body,
        out_shape=[jax.ShapeDtypeStruct((rows, cols, width), BF16)] + flush.shapes(shape),
        in_specs=[SMEM] * len(flags) + [VMEM] * 2 + flush.specs(),
        out_specs=[VMEM] + [HBM] * bool(more),
        scratch_shapes=flush.scratch(),
        input_output_aliases=flush.aliases(inputs, 1),
        compiler_params=params(8),
        cost_estimate=conv_cost(rows, cols, width),
    )(*flags, window, weights, *more)
    if more:
        flush.outputs[flush.name] = results[1]
    flush.piece, flush.first, flush.name = results[0], first, name


def turn_group(wide):
    return 128 // math.gcd(128, wide)


def begin_kernel(field_hbm, cot_hbm, columns, window, turned, sums, cot, field, column_rows, sems):
    total, cols, width = field.shape
    wide = padded_width(cols)
    part = 2 * turn_group(wide)
    chunks = -(-total // part)
    sizes = [min(part, total - at) for at in range(0, total, part)]

    def copies(i, size):
        at = i * part
        return [
            pltpu.make_async_copy(source.at[pl.ds(at, size)], target.at[pl.ds(at, size)], sems.at[i, j])
            for j, (source, target) in enumerate(((field_hbm, field), (cot_hbm, cot)))
        ]

    for i, size in enumerate(sizes):
        for copy in copies(i, size):
            copy.start()
    empty = jnp.zeros((1, width), F32)
    blank = jnp.zeros((wide - cols, width), F32)
    for k in range(3):
        window[0:wide, k * width : (k + 1) * width] = jnp.zeros((wide, width), BF16)
        window[(total + 1) * wide : (total + 2) * wide, k * width : (k + 1) * width] = jnp.zeros((wide, width), BF16)
    sums[...] = jnp.zeros_like(sums)

    def lay(i, size):
        for copy in copies(i, size):
            copy.wait()
        step = size if size % 2 else size // 2
        for low in range(0, size, step):
            flat = []
            for u in range(low, low + step):
                r = i * part + u
                row, other = field[r], cot[r].astype(F32)
                start = pl.multiple_of((r + 1) * wide, 16)
                for tap, piece in enumerate(shifted(row, empty, empty, wide)):
                    window[pl.ds(start, wide), tap * width : (tap + 1) * width] = piece
                row = row.astype(F32)
                for k, value in enumerate((row[0:1], row[cols - 1 : cols], other[0:1], other[cols - 1 : cols])):
                    column_rows[k, pl.ds(r, 1)] = value
                flat += [other, blank]
            value = jnp.concatenate(flat, 0).T.astype(BF16)
            if step * wide % 128 == 0:
                at = pl.multiple_of((i * part + low) * wide, 128)
                turned[:, pl.ds(at, step * wide)] = value
            else:
                turned[:, (i * part + low) * wide : (i * part + low + step) * wide] = value

    def multiply(i, size):
        at = i * part * wide
        at = at if isinstance(at, int) else pl.multiple_of(at, 128)
        sums[...] += jnp.dot(
            turned[:, pl.ds(at, size * wide)],
            window[pl.ds(at + wide, size * wide), :],
            preferred_element_type=F32,
        )

    lay(0, sizes[0])

    @pl.loop(1, chunks - 1)
    def _(i):
        lay(i, part)
        multiply(i - 1, part)

    if chunks > 1:
        lay(chunks - 1, sizes[-1])
        multiply(chunks - 2, part)
    multiply(chunks - 1, sizes[-1])
    columns[...] = column_rows[...].astype(BF16)


def store_turned(value, taps, slot):
    width = taps.shape[-1]
    for b in range(3):
        taps[slot + b] = value[:, b * width : (b + 1) * width].T


def begin(field, cot):
    total, cols, width = field.shape
    wide = padded_width(cols)
    group = turn_group(wide)
    return pl.pallas_call(
        begin_kernel,
        out_shape=(
            jax.ShapeDtypeStruct((4, total, width), BF16),
            jax.ShapeDtypeStruct(((total + 2) * wide, 3 * width), BF16),
            jax.ShapeDtypeStruct((width, -(-total // group) * group * wide), BF16),
            jax.ShapeDtypeStruct((width, 3 * width), F32),
            jax.ShapeDtypeStruct(cot.shape, BF16),
        ),
        in_specs=[HBM, HBM],
        out_specs=(VMEM,) * 5,
        scratch_shapes=[
            pltpu.VMEM(field.shape, BF16),
            pltpu.VMEM((4, total, width), F32),
            pltpu.SemaphoreType.DMA((-(-total // (2 * group)), 2)),
        ],
        compiler_params=params(12),
        cost_estimate=pl.CostEstimate(
            flops=8 * total * wide * width * width, bytes_accessed=4 * total * wide * width, transcendentals=0
        ),
    )(field, cot)


def flip(kernel):
    width = kernel.shape[-1]

    def body(kernel, out):
        for tap in range(9):
            a, b = divmod(tap, 3)
            out[a, b * width : (b + 1) * width] = kernel[2 - a, 2 - b].astype(F32).T.astype(BF16)

    return pl.pallas_call(
        body,
        out_shape=jax.ShapeDtypeStruct((3, 3 * width, width), BF16),
        in_specs=[VMEM],
        out_specs=VMEM,
        compiler_params=params(8),
        cost_estimate=pl.CostEstimate(flops=0, bytes_accessed=36 * width * width, transcendentals=0),
    )(kernel)


def all_taps(window, turned, middle, total, wide):
    width = turned.shape[0]
    cells = total * wide

    def body(window, turned, middle, taps):
        store_turned(middle[...], taps, 3)
        for slot, start in ((0, 0), (6, 2 * wide)):
            store_turned(
                jnp.dot(turned[:, :cells], window[start : start + cells, :], preferred_element_type=F32), taps, slot
            )

    return pl.pallas_call(
        body,
        out_shape=jax.ShapeDtypeStruct((9, width, width), F32),
        in_specs=[VMEM] * 3,
        out_specs=VMEM,
        compiler_params=params(8),
        cost_estimate=pl.CostEstimate(
            flops=12 * total * wide * width * width, bytes_accessed=4 * total * wide * width, transcendentals=0
        ),
    )(window, turned, middle)


def edge_kernel(half, taps, ends, sides, rows, columns, send, every, side_rows):
    _, cols, width = ends.shape
    wide = padded_width(cols)
    total = columns.shape[1]
    tall = -(-total // 16) * 16
    side_rows[...] = sides[...].astype(F32)
    empty = jnp.zeros((1, width), F32)
    end_parts = [shifted(ends[k], empty, empty, wide) for k in range(2)]
    blank = jnp.zeros((wide - cols, width), F32)
    row_parts = [jnp.concatenate([rows[k].astype(F32), blank], 0).astype(BF16) for k in range(2)]
    low = jnp.zeros((tall - total, width), F32)
    column_parts = [jnp.concatenate([columns[k].astype(F32), low], 0).astype(BF16) for k in range(2)]
    size = 9 * width // 2
    for tap in range(9):
        a, b = divmod(tap, 3)
        left, right = [], []
        if b != 1:
            side = b // 2
            left.append(jnp.concatenate([side_rows[side, a : a + total], low], 0).astype(BF16))
            right.append(column_parts[side])
        if a != 1:
            left.append(end_parts[a // 2][b])
            right.append(row_parts[a // 2])
        value = taps[tap]
        if left:
            value = value + lax.dot_general(
                jnp.concatenate(left, 0),
                jnp.concatenate(right, 0),
                (((0,), (0,)), ((), ())),
                preferred_element_type=F32,
            )
        every[tap * width : (tap + 1) * width] = value
    send[...] = every[pl.ds(pl.multiple_of((1 - half[0]) * size, 8), size)]


def with_edges(half, taps, ends, sides, rows, columns):
    _, _, width = ends.shape
    total = columns.shape[1]
    return pl.pallas_call(
        edge_kernel,
        out_shape=(
            jax.ShapeDtypeStruct((9 * width // 2, width), F32),
            jax.ShapeDtypeStruct((9 * width, width), F32),
        ),
        in_specs=[SMEM] + [VMEM] * 5,
        out_specs=(VMEM, VMEM),
        scratch_shapes=[pltpu.VMEM((2, total + 2, width), F32)],
        compiler_params=params(12),
        cost_estimate=pl.CostEstimate(
            flops=16 * 144 * width * width, bytes_accessed=72 * width * width, transcendentals=0
        ),
    )(half, taps, ends, sides, rows, columns)


def add_blocks(places, terms, sizes):
    width = terms[0].shape[1]
    count = len(sizes)

    def body(where, *refs):
        sources, outs = refs[: len(terms)], refs[len(terms) :]
        for k, size in enumerate(sizes):
            value = None
            for t, source in enumerate(sources):
                part = source[pl.ds(pl.multiple_of(where[t * count + k], 8), size)]
                value = part if value is None else value + part
            outs[k][...] = value

    return pl.pallas_call(
        body,
        out_shape=tuple(jax.ShapeDtypeStruct((size, width), F32) for size in sizes),
        in_specs=[SMEM] + [VMEM] * len(terms),
        out_specs=(VMEM,) * count,
        compiler_params=params(8),
        cost_estimate=pl.CostEstimate(
            flops=sum(sizes) * width, bytes_accessed=4 * sum(sizes) * width * (len(terms) + 1), transcendentals=0
        ),
    )(places, *terms)


def join_sums(upper, lower):
    above, width = upper[0].shape
    below = lower[0].shape[0]

    def body(*refs):
        out = refs[-1]
        for at, size, sources in ((0, above, refs[: len(upper)]), (above, below, refs[len(upper) : -1])):
            value = sources[0][...]
            for source in sources[1:]:
                value = value + source[...]
            out[at : at + size] = value

    return pl.pallas_call(
        body,
        out_shape=jax.ShapeDtypeStruct((above + below, width), F32),
        in_specs=[VMEM] * (len(upper) + len(lower)),
        out_specs=VMEM,
        compiler_params=params(8),
        cost_estimate=pl.CostEstimate(
            flops=4 * (above + below) * width, bytes_accessed=16 * (above + below) * width, transcendentals=0
        ),
    )(*upper, *lower)


def last_sum(terms, scale):
    rows, width = terms[0].shape

    def body(first, second, out):
        value = (first[...] + second[...]) * scale
        top = jnp.max(jnp.max(jnp.abs(value), axis=1, keepdims=True), axis=0, keepdims=True)
        exponent = jnp.ceil(jnp.log2(jnp.maximum(top, 1e-30)))
        out[:rows] = value * jnp.exp2(-exponent)
        out[rows:] = jnp.broadcast_to(exponent, (8, width))

    return pl.pallas_call(
        body,
        out_shape=jax.ShapeDtypeStruct((rows + 8, width), F32),
        in_specs=[VMEM] * 2,
        out_specs=VMEM,
        compiler_params=params(8),
        cost_estimate=pl.CostEstimate(flops=8 * rows * width, bytes_accessed=12 * rows * width, transcendentals=0),
    )(*terms)


def decode(coded):
    return coded[..., :-8, :].astype(F32) * jnp.exp2(coded[..., -1:, :].astype(F32))


def put_blocks(places, blocks, cuts, total, out=None, flush=None, shape=None):
    count, _, width = blocks.shape
    more = [] if out is None else [out]
    late = [] if flush is None else flush.operands()
    inputs = 2 + len(more)

    def body(where, blocks, *rest):
        refs = rest[len(more) + len(late) :]
        out, sem = refs[0], refs[-1]
        copy = None
        if late:
            copy = flush.copy(rest[len(more)], refs[1], refs[2])
            copy.start()
        for k in range(count):
            start = 0
            for j, size in enumerate(cuts):
                at = pl.multiple_of(where[2 * k + j], 8)
                pltpu.make_async_copy(blocks.at[k, pl.ds(start, size)], out.at[pl.ds(at, size)], sem).start()
                start += size
        pltpu.make_async_copy(blocks, blocks, sem).wait()
        if copy is not None:
            copy.wait()

    results = pl.pallas_call(
        body,
        out_shape=[jax.ShapeDtypeStruct((total, width), F32)] + (flush.shapes(shape) if late else []),
        in_specs=[SMEM, VMEM] + [HBM] * len(more) + (flush.specs() if late else []),
        out_specs=[HBM] * (1 + bool(late)),
        scratch_shapes=(flush.scratch() if late else []) + [pltpu.SemaphoreType.DMA],
        input_output_aliases={**({2: 0} if more else {}), **(flush.aliases(inputs, 1) if late else {})},
        compiler_params=params(8),
    )(places, blocks, *more, *late)
    if late:
        flush.outputs[flush.name] = results[1]
    return results[0]


def swap(value, axis, mask):
    count = lax.axis_size(axis)
    return lax.ppermute(value, axis, [(i, i ^ mask) for i in range(count)])


def swap_next(value, axis):
    count = lax.axis_size(axis)
    return lax.ppermute(value, axis, [(i, (i + (1 if i % 2 else -1)) % count) for i in range(count)])


def swap_rows(value):
    bands, sectors = lax.axis_size("lat"), lax.axis_size("lon")
    pairs = []
    for band in range(bands):
        for sector in range(sectors):
            if band == 0 or band == bands - 1:
                other = (band, (sector + sectors // 2) % sectors)
            else:
                other = (band + (1 if band % 2 else -1), sector)
            pairs.append((band * sectors + sector, other[0] * sectors + other[1]))
    return lax.ppermute(value, ("lat", "lon"), pairs)


def local(inputs, kernel, cotangent):
    rows, cols, width = inputs.shape
    bands, sectors = lax.axis_size("lat"), lax.axis_size("lon")
    band, sector = lax.axis_index("lat"), lax.axis_index("lon")

    def vector(*values):
        return jnp.stack([jnp.asarray(v, jnp.int32) for v in values])

    mine, place = sector & 1, (sector >> 1) & 1
    odd = band & 1
    half_rows = 9 * width // 2
    unit = 16 * bands
    upper = half_rows * 5 // 8 // unit * unit
    lower = half_rows - upper
    upper_part, lower_part = upper // bands, lower // 2
    upper_end, lower_end = upper_part // 2, lower_part // bands
    first_sizes = [upper_part] * bands + [lower_part] * 2
    first_rows = [(band ^ m) * upper_part for m in range(bands)]
    first_rows += [upper + p * lower_part for p in (place, 1 - place)]

    def homes(h, p):
        return vector(
            *[
                h * half_rows + row
                for m in range(bands)
                for row in (
                    (band ^ m) * upper_part + p * upper_end,
                    upper + p * lower_part + (band ^ m) * lower_end,
                )
            ]
        )

    facts = dict(
        even_band=odd == 0,
        even_sector=mine == 0,
        half=vector(mine),
        near_row=(1 - odd) * (rows - 1),
        far_row=odd * (rows - 1),
        first=vector(*[mine * half_rows + row for row in first_rows], *first_rows),
        upper=vector(*[p * upper_end for _ in range(bands) for p in (place, 1 - place)]),
        lower=vector(*[(band ^ m) * lower_end for _ in range(2) for m in range(bands)]),
        poles=vector(jnp.where(band == 0, 2, 0), jnp.where(band == bands - 1, 0, 2)),
        most_homes=jnp.concatenate([homes(mine, place), homes(mine, 1 - place), homes(1 - mine, place)]),
        last_homes=homes(1 - mine, 1 - place),
    )
    inputs, kernel, cotangent, facts = lax.optimization_barrier((inputs, kernel, cotangent, facts))
    even_band, even_sector, half = facts["even_band"], facts["even_sector"], facts["half"]

    near, far = (
        jnp.stack([lax.dynamic_index_in_dim(field, facts[name], 0, False) for field in (inputs, cotangent)])
        for name in ("near_row", "far_row")
    )
    near = swap(near, "lat", 1)
    far = swap_rows(far)
    columns, window, turned, middle, cot = begin(in_hbm(inputs), in_hbm(cotangent))
    ends = jnp.stack([jnp.where(even_band, far, near), jnp.where(even_band, near, far)], 1)

    def side(place):
        column = 0 if place == 0 else cols - 1
        return jnp.stack(
            [
                jnp.concatenate([ends[k, :1, column], columns[2 * k + place], ends[k, 1:, column]], 0)
                for k in range(2)
            ]
        )

    first, last = side(0), side(1)
    near = swap(jnp.where(even_sector, last, first), "lon", 1)
    far = swap_next(jnp.where(even_sector, first, last), "lon")
    outer = all_taps(window, turned, middle, rows, padded_width(cols))
    sides = jnp.stack([jnp.where(even_sector, far, near), jnp.where(even_sector, near, far)], 1)

    edge_rows = jnp.stack([cotangent[0], cotangent[-1]])
    send, every = with_edges(half, outer, ends[0], sides[0], edge_rows, columns[2:])

    weights = kernel.reshape(3, 3 * width, width)
    flipped = flip(kernel)
    window = patch(window, ends[0], sides[0])
    cot_window = prepare(cot, ends[1], sides[1])
    flush = Flush()
    for name, (start, count) in pieces(rows):
        if name.startswith("forward"):
            conv(None, window, weights, inputs.shape, start, count, "outputs", flush)
        else:
            conv(facts["poles"], cot_window, flipped, inputs.shape, start, count, "input_grad", flush)

    got = swap(send, "lon", 1)
    *parts, low_keep, low_send = add_blocks(facts["first"], [every, got], first_sizes)
    low_got = swap(low_send, "lon", 2)
    got = []
    for m in range(1, bands):
        got.append(swap(parts[m], "lat", m))
    lows = add_blocks(facts["lower"], [low_keep, low_got], [lower_end] * bands)
    keep, send = add_blocks(facts["upper"], [parts[0], *got], [upper_end] * 2)
    low_got = []
    got = swap(send, "lon", 2)
    for m in range(1, bands):
        low_got.append(swap(lows[m], "lat", m))
    value = join_sums([keep, got], [lows[0], *low_got])
    factor = 1.0 / math.sqrt(rows * cols * bands * sectors)
    mask = 4
    while mask < sectors:
        terms = [value, swap(value, "lon", mask)]
        mask *= 2
        if mask < sectors:
            value = terms[0] + terms[1]

    coded = last_sum(terms, factor).astype(HALF)
    other = swap(coded, "lon", 2)
    whole, cuts = 9 * width, (upper_end, lower_end)

    def spread(value):
        got = []
        for m in range(1, bands):
            got.append(swap(value, "lat", m))
        return [value, *got]

    near = spread(coded)
    far = spread(other)
    near = jnp.stack(near)
    near_other = swap(near, "lon", 1)
    near_blocks = decode(near)
    far = jnp.stack(far)
    far_other = swap(far, "lon", 1)
    most = jnp.concatenate([near_blocks, decode(far), decode(near_other)])
    kernel_grad = put_blocks(facts["most_homes"], most, cuts, whole, None, flush, inputs.shape)
    kernel_grad = put_blocks(facts["last_homes"], decode(far_other), cuts, whole, kernel_grad)
    return (flush.outputs["outputs"], flush.outputs["input_grad"], kernel_grad.reshape(3, 3, width, width))


PIECES = (
    ("forward_0", 0, 45),
    ("forward_1", 45, 75),
    ("backward_0", 0, 75),
    ("forward_2", 75, 90),
    ("backward_1", 75, 90),
)


def pieces(rows):
    if max(high for _, _, high in PIECES) != rows:
        return [("forward_0", (0, rows)), ("backward_0", (0, rows))]
    return [(name, (low, high - low)) for name, low, high in PIECES]


def solution(mesh):
    in_specs = (P("lat", "lon", None), P(), P("lat", "lon", None))
    out_specs = (P("lat", "lon", None), P("lat", "lon", None), P())
    return jax.shard_map(local, mesh=mesh, in_specs=in_specs, out_specs=out_specs, check_vma=False)
```

```python
import math

import jax
import jax.numpy as jnp
from jax import lax
from jax.experimental import pallas as pl
from jax.experimental.pallas import tpu as pltpu
from jax.sharding import PartitionSpec as P


F32 = jnp.float32
BF16 = jnp.bfloat16
HALF = jnp.float16
VMEM = pl.BlockSpec(memory_space=pltpu.VMEM)
SMEM = pl.BlockSpec(memory_space=pltpu.SMEM)
HBM = pl.BlockSpec(memory_space=pltpu.HBM)


def padded_width(cols):
    return -(-(cols + 3) // 16) * 16


def in_hbm(value):
    return pltpu.with_memory_space_constraint(value, pltpu.HBM)


def spot():
    sector = lax.axis_index("lon")
    return lax.axis_index("lat"), sector & 1, (sector >> 1) & 1


def params(mib):
    return pltpu.CompilerParams(vmem_limit_bytes=mib << 20)


def shifted(row, left, right, wide):
    cols, width = row.shape
    middle = jnp.zeros((wide - cols - 2, width), F32)
    base = jnp.concatenate([row.astype(F32), right, middle, left], 0)
    return (
        pltpu.roll(base, 1, 0).astype(BF16),
        base.astype(BF16),
        pltpu.roll(base, wide - 1, 0).astype(BF16),
    )


def fill_window(field, ends, sides, side_rows, window, first, rows):
    total, cols, width = field.shape
    wide = padded_width(cols)
    side_rows[...] = sides[...].astype(F32)

    def put(slot, row, at):
        parts = shifted(row, side_rows[0, pl.ds(at, 1)], side_rows[1, pl.ds(at, 1)], wide)
        start = slot * wide if isinstance(slot, int) else pl.multiple_of(slot * wide, 16)
        for tap, part in enumerate(parts):
            window[pl.ds(start, wide), tap * width : (tap + 1) * width] = part

    low = 0
    if first == 0:
        put(0, ends[0], 0)
        low = 1
    high = rows + 2
    if first + rows == total:
        put(rows + 1, ends[1], total + 1)
        high = rows + 1

    @pl.loop(low, high)
    def _(slot):
        put(slot, field[first + slot - 1], first + slot)


def block_rows(rows):
    return max(n for n in range(1, 6) if rows % n == 0)


def conv_rows(taps, window, weights, result, cols, first, rows, total):
    width = weights.shape[-1]
    wide = padded_width(cols)
    step = block_rows(rows)

    def term(slot, count, which):
        at = slot * wide if isinstance(slot, int) else pl.multiple_of(slot * wide, 16)
        return jnp.dot(window[pl.ds(at, count * wide), :], weights[which], preferred_element_type=F32)

    def block(i, top=0, bottom=2):
        start = i * step
        if isinstance(top, int):
            value = term(start, step, 0)
        else:
            value = jnp.concatenate([term(start, 1, top), term(start + 1, step - 1, 0)], 0)
        value = value + term(start + 1, step, 1)
        if isinstance(bottom, int):
            value = value + term(start + 2, step, 2)
        else:
            value = value + jnp.concatenate(
                [term(start + 2, step - 1, 2), term(start + step + 1, 1, bottom)], 0
            )
        result[pl.ds(start, step)] = value.reshape(step, wide, width)[:, :cols].astype(BF16)

    count = rows // step
    poles = taps is not None and step > 1
    low = int(first == 0 and poles)
    high = count - int(first + rows == total and poles)
    group = 3
    trips = (high - low) // group

    @pl.loop(0, trips)
    def _(j):
        for u in range(group):
            block(low + j * group + u)

    for i in range(low + trips * group, high):
        block(i)
    if low:
        block(0, top=taps[0])
    if high < count:
        block(count - 1, bottom=taps[1])


def conv_cost(rows, cols, width):
    wide = padded_width(cols)
    return pl.CostEstimate(
        flops=18 * rows * wide * width * width, bytes_accessed=4 * rows * wide * width, transcendentals=0
    )


def prepare(field, ends, sides):
    total, cols, width = field.shape
    wide = padded_width(cols)

    def body(field, ends, sides, window, side_rows):
        fill_window(field, ends, sides, side_rows, window, 0, total)

    return pl.pallas_call(
        body,
        out_shape=jax.ShapeDtypeStruct(((total + 2) * wide, 3 * width), BF16),
        in_specs=[VMEM] * 3,
        out_specs=VMEM,
        scratch_shapes=[pltpu.VMEM((2, total + 2, width), F32)],
        compiler_params=params(8),
        cost_estimate=pl.CostEstimate(flops=0, bytes_accessed=8 * total * wide * width, transcendentals=0),
    )(field, ends, sides)


def patch(window, ends, sides):
    _, cols, width = ends.shape
    wide = padded_width(cols)
    total = sides.shape[1] - 2

    def body(old, ends, sides, window, side_rows):
        side_rows[...] = sides[...].astype(F32)
        for slot, k in ((0, 0), (total + 1, 1)):
            parts = shifted(ends[k], side_rows[0, slot : slot + 1], side_rows[1, slot : slot + 1], wide)
            for tap, part in enumerate(parts):
                window[slot * wide : (slot + 1) * wide, tap * width : (tap + 1) * width] = part
        place = lax.broadcasted_iota(jnp.int32, (16, width), 0)
        last = (cols - 1) // 16 * 16

        @pl.loop(1, total + 1)
        def _(slot):
            for k, (offset, at) in enumerate(((0, 0), (last, cols - 1 - last))):
                where = (pl.ds(pl.multiple_of(slot * wide + offset, 16), 16), slice(2 * k * width, (2 * k + 1) * width))
                value = window[where].astype(F32)
                window[where] = jnp.where(place == at, side_rows[k, pl.ds(slot, 1)], value).astype(BF16)

    return pl.pallas_call(
        body,
        out_shape=jax.ShapeDtypeStruct(window.shape, BF16),
        in_specs=[VMEM] * 3,
        out_specs=VMEM,
        scratch_shapes=[pltpu.VMEM((2, total + 2, width), F32)],
        input_output_aliases={0: 0},
        compiler_params=params(8),
        cost_estimate=pl.CostEstimate(flops=0, bytes_accessed=256 * total * width, transcendentals=0),
    )(window, ends, sides)


class Flush:
    def __init__(self):
        self.piece = self.first = self.name = None
        self.outputs = {}

    def operands(self):
        if self.piece is None:
            return []
        known = self.outputs.get(self.name)
        return [self.piece] if known is None else [self.piece, known]

    def specs(self):
        return [VMEM, HBM][: len(self.operands())]

    def shapes(self, shape):
        return [] if self.piece is None else [jax.ShapeDtypeStruct(shape, BF16)]

    def aliases(self, operand, output):
        return {operand + 1: output} if len(self.operands()) == 2 else {}

    def scratch(self):
        return [] if self.piece is None else [pltpu.SemaphoreType.DMA]

    def copy(self, piece, out, sem):
        return pltpu.make_async_copy(piece, out.at[pl.ds(self.first, self.piece.shape[0])], sem)


def conv(taps, window, weights, shape, first, rows, name, flush):
    total, cols, width = shape
    wide = padded_width(cols)
    more = flush.operands()
    inputs = 2

    def body(*refs):
        window, weights = refs[:inputs]
        result = refs[inputs + len(more)]
        copy = None
        if more:
            copy = flush.copy(refs[inputs], refs[-2], refs[-1])
            copy.start()
        view = window.at[first * wide : (first + rows + 2) * wide]
        conv_rows(taps and taps(), view, weights, result, cols, first, rows, total)
        if copy is not None:
            copy.wait()

    results = pl.pallas_call(
        body,
        out_shape=[jax.ShapeDtypeStruct((rows, cols, width), BF16)] + flush.shapes(shape),
        in_specs=[VMEM] * 2 + flush.specs(),
        out_specs=[VMEM] + [HBM] * bool(more),
        scratch_shapes=flush.scratch(),
        input_output_aliases=flush.aliases(inputs, 1),
        compiler_params=params(8),
        cost_estimate=conv_cost(rows, cols, width),
    )(window, weights, *more)
    if more:
        flush.outputs[flush.name] = results[1]
    flush.piece, flush.first, flush.name = results[0], first, name


def turn_group(wide):
    return 128 // math.gcd(128, wide)


def begin_kernel(field_hbm, cot_hbm, columns, window, turned, sums, cot, field, column_rows, sems):
    total, cols, width = field.shape
    wide = padded_width(cols)
    part = 2 * turn_group(wide)
    chunks = -(-total // part)
    sizes = [min(part, total - at) for at in range(0, total, part)]

    def copies(i, size):
        at = i * part
        return [
            pltpu.make_async_copy(source.at[pl.ds(at, size)], target.at[pl.ds(at, size)], sems.at[i, j])
            for j, (source, target) in enumerate(((field_hbm, field), (cot_hbm, cot)))
        ]

    for i, size in enumerate(sizes):
        for copy in copies(i, size):
            copy.start()
    empty = jnp.zeros((1, width), F32)
    blank = jnp.zeros((wide - cols, width), F32)
    for k in range(3):
        window[0:wide, k * width : (k + 1) * width] = jnp.zeros((wide, width), BF16)
        window[(total + 1) * wide : (total + 2) * wide, k * width : (k + 1) * width] = jnp.zeros((wide, width), BF16)
    sums[...] = jnp.zeros_like(sums)

    def lay(i, size):
        for copy in copies(i, size):
            copy.wait()
        step = size if size % 2 else size // 2
        for low in range(0, size, step):
            flat = []
            for u in range(low, low + step):
                r = i * part + u
                row, other = field[r], cot[r].astype(F32)
                start = pl.multiple_of((r + 1) * wide, 16)
                for tap, piece in enumerate(shifted(row, empty, empty, wide)):
                    window[pl.ds(start, wide), tap * width : (tap + 1) * width] = piece
                row = row.astype(F32)
                for k, value in enumerate((row[0:1], row[cols - 1 : cols], other[0:1], other[cols - 1 : cols])):
                    column_rows[k, pl.ds(r, 1)] = value
                flat += [other, blank]
            value = jnp.concatenate(flat, 0).T.astype(BF16)
            if step * wide % 128 == 0:
                at = pl.multiple_of((i * part + low) * wide, 128)
                turned[:, pl.ds(at, step * wide)] = value
            else:
                turned[:, (i * part + low) * wide : (i * part + low + step) * wide] = value

    def multiply(i, size):
        at = i * part * wide
        at = at if isinstance(at, int) else pl.multiple_of(at, 128)
        sums[...] += jnp.dot(
            turned[:, pl.ds(at, size * wide)],
            window[pl.ds(at + wide, size * wide), :],
            preferred_element_type=F32,
        )

    lay(0, sizes[0])

    @pl.loop(1, chunks - 1)
    def _(i):
        lay(i, part)
        multiply(i - 1, part)

    if chunks > 1:
        lay(chunks - 1, sizes[-1])
        multiply(chunks - 2, part)
    multiply(chunks - 1, sizes[-1])
    columns[...] = column_rows[...].astype(BF16)


def store_turned(value, taps, slot):
    width = taps.shape[-1]
    for b in range(3):
        taps[slot + b] = value[:, b * width : (b + 1) * width].T


def begin(field, cot):
    total, cols, width = field.shape
    wide = padded_width(cols)
    group = turn_group(wide)
    return pl.pallas_call(
        begin_kernel,
        out_shape=(
            jax.ShapeDtypeStruct((4, total, width), BF16),
            jax.ShapeDtypeStruct(((total + 2) * wide, 3 * width), BF16),
            jax.ShapeDtypeStruct((width, -(-total // group) * group * wide), BF16),
            jax.ShapeDtypeStruct((width, 3 * width), F32),
            jax.ShapeDtypeStruct(cot.shape, BF16),
        ),
        in_specs=[HBM, HBM],
        out_specs=(VMEM,) * 5,
        scratch_shapes=[
            pltpu.VMEM(field.shape, BF16),
            pltpu.VMEM((4, total, width), F32),
            pltpu.SemaphoreType.DMA((-(-total // (2 * group)), 2)),
        ],
        compiler_params=params(12),
        cost_estimate=pl.CostEstimate(
            flops=8 * total * wide * width * width, bytes_accessed=4 * total * wide * width, transcendentals=0
        ),
    )(field, cot)


def flip(kernel):
    width = kernel.shape[-1]

    def body(kernel, out):
        for tap in range(9):
            a, b = divmod(tap, 3)
            out[a, b * width : (b + 1) * width] = kernel[2 - a, 2 - b].astype(F32).T.astype(BF16)

    return pl.pallas_call(
        body,
        out_shape=jax.ShapeDtypeStruct((3, 3 * width, width), BF16),
        in_specs=[VMEM],
        out_specs=VMEM,
        compiler_params=params(8),
        cost_estimate=pl.CostEstimate(flops=0, bytes_accessed=36 * width * width, transcendentals=0),
    )(kernel)


def all_taps(window, turned, middle, total, wide):
    width = turned.shape[0]
    cells = total * wide

    def body(window, turned, middle, taps):
        store_turned(middle[...], taps, 3)
        for slot, start in ((0, 0), (6, 2 * wide)):
            store_turned(
                jnp.dot(turned[:, :cells], window[start : start + cells, :], preferred_element_type=F32), taps, slot
            )

    return pl.pallas_call(
        body,
        out_shape=jax.ShapeDtypeStruct((9, width, width), F32),
        in_specs=[VMEM] * 3,
        out_specs=VMEM,
        compiler_params=params(8),
        cost_estimate=pl.CostEstimate(
            flops=12 * total * wide * width * width, bytes_accessed=4 * total * wide * width, transcendentals=0
        ),
    )(window, turned, middle)


def edge_kernel(taps, ends, sides, rows, columns, send, every, side_rows):
    _, cols, width = ends.shape
    wide = padded_width(cols)
    total = columns.shape[1]
    tall = -(-total // 16) * 16
    side_rows[...] = sides[...].astype(F32)
    empty = jnp.zeros((1, width), F32)
    end_parts = [shifted(ends[k], empty, empty, wide) for k in range(2)]
    blank = jnp.zeros((wide - cols, width), F32)
    row_parts = [jnp.concatenate([rows[k].astype(F32), blank], 0).astype(BF16) for k in range(2)]
    low = jnp.zeros((tall - total, width), F32)
    column_parts = [jnp.concatenate([columns[k].astype(F32), low], 0).astype(BF16) for k in range(2)]
    size = 9 * width // 2
    for tap in range(9):
        a, b = divmod(tap, 3)
        left, right = [], []
        if b != 1:
            side = b // 2
            left.append(jnp.concatenate([side_rows[side, a : a + total], low], 0).astype(BF16))
            right.append(column_parts[side])
        if a != 1:
            left.append(end_parts[a // 2][b])
            right.append(row_parts[a // 2])
        value = taps[tap]
        if left:
            value = value + lax.dot_general(
                jnp.concatenate(left, 0),
                jnp.concatenate(right, 0),
                (((0,), (0,)), ((), ())),
                preferred_element_type=F32,
            )
        every[tap * width : (tap + 1) * width] = value
    send[...] = every[pl.ds(pl.multiple_of((1 - spot()[1]) * size, 8), size)]


def with_edges(taps, ends, sides, rows, columns):
    _, _, width = ends.shape
    total = columns.shape[1]
    return pl.pallas_call(
        edge_kernel,
        out_shape=(
            jax.ShapeDtypeStruct((9 * width // 2, width), F32),
            jax.ShapeDtypeStruct((9 * width, width), F32),
        ),
        in_specs=[VMEM] * 5,
        out_specs=(VMEM, VMEM),
        scratch_shapes=[pltpu.VMEM((2, total + 2, width), F32)],
        compiler_params=params(12),
        cost_estimate=pl.CostEstimate(
            flops=16 * 144 * width * width, bytes_accessed=72 * width * width, transcendentals=0
        ),
    )(taps, ends, sides, rows, columns)


def add_blocks(places, terms, sizes):
    width = terms[0].shape[1]
    count = len(sizes)

    def body(*refs):
        where = places(*spot())
        sources, outs = refs[: len(terms)], refs[len(terms) :]
        for k, size in enumerate(sizes):
            value = None
            for t, source in enumerate(sources):
                part = source[pl.ds(pl.multiple_of(where[t * count + k], 8), size)]
                value = part if value is None else value + part
            outs[k][...] = value

    return pl.pallas_call(
        body,
        out_shape=tuple(jax.ShapeDtypeStruct((size, width), F32) for size in sizes),
        in_specs=[VMEM] * len(terms),
        out_specs=(VMEM,) * count,
        compiler_params=params(8),
        cost_estimate=pl.CostEstimate(
            flops=sum(sizes) * width, bytes_accessed=4 * sum(sizes) * width * (len(terms) + 1), transcendentals=0
        ),
    )(*terms)


def join_sums(upper, lower):
    above, width = upper[0].shape
    below = lower[0].shape[0]

    def body(*refs):
        out = refs[-1]
        for at, size, sources in ((0, above, refs[: len(upper)]), (above, below, refs[len(upper) : -1])):
            value = sources[0][...]
            for source in sources[1:]:
                value = value + source[...]
            out[at : at + size] = value

    return pl.pallas_call(
        body,
        out_shape=jax.ShapeDtypeStruct((above + below, width), F32),
        in_specs=[VMEM] * (len(upper) + len(lower)),
        out_specs=VMEM,
        compiler_params=params(8),
        cost_estimate=pl.CostEstimate(
            flops=4 * (above + below) * width, bytes_accessed=16 * (above + below) * width, transcendentals=0
        ),
    )(*upper, *lower)


def last_sum(terms, scale):
    rows, width = terms[0].shape

    def body(first, second, out):
        value = (first[...] + second[...]) * scale
        top = jnp.max(jnp.max(jnp.abs(value), axis=1, keepdims=True), axis=0, keepdims=True)
        exponent = jnp.ceil(jnp.log2(jnp.maximum(top, 1e-30)))
        out[:rows] = value * jnp.exp2(-exponent)
        out[rows:] = jnp.broadcast_to(exponent, (8, width))

    return pl.pallas_call(
        body,
        out_shape=jax.ShapeDtypeStruct((rows + 8, width), F32),
        in_specs=[VMEM] * 2,
        out_specs=VMEM,
        compiler_params=params(8),
        cost_estimate=pl.CostEstimate(flops=8 * rows * width, bytes_accessed=12 * rows * width, transcendentals=0),
    )(*terms)


def decode(coded):
    return coded[..., :-8, :].astype(F32) * jnp.exp2(coded[..., -1:, :].astype(F32))


def put_blocks(places, blocks, cuts, total, out=None, flush=None, shape=None):
    count, _, width = blocks.shape
    more = [] if out is None else [out]
    late = [] if flush is None else flush.operands()
    inputs = 1 + len(more)

    def body(blocks, *rest):
        where = places(*spot())
        refs = rest[len(more) + len(late) :]
        out, sem = refs[0], refs[-1]
        copy = None
        if late:
            copy = flush.copy(rest[len(more)], refs[1], refs[2])
            copy.start()
        for k in range(count):
            start = 0
            for j, size in enumerate(cuts):
                at = pl.multiple_of(where[2 * k + j], 8)
                pltpu.make_async_copy(blocks.at[k, pl.ds(start, size)], out.at[pl.ds(at, size)], sem).start()
                start += size
        pltpu.make_async_copy(blocks, blocks, sem).wait()
        if copy is not None:
            copy.wait()

    results = pl.pallas_call(
        body,
        out_shape=[jax.ShapeDtypeStruct((total, width), F32)] + (flush.shapes(shape) if late else []),
        in_specs=[VMEM] + [HBM] * len(more) + (flush.specs() if late else []),
        out_specs=[HBM] * (1 + bool(late)),
        scratch_shapes=(flush.scratch() if late else []) + [pltpu.SemaphoreType.DMA],
        input_output_aliases={**({1: 0} if more else {}), **(flush.aliases(inputs, 1) if late else {})},
        compiler_params=params(8),
    )(blocks, *more, *late)
    if late:
        flush.outputs[flush.name] = results[1]
    return results[0]


def swap(value, axis, mask):
    count = lax.axis_size(axis)
    return lax.ppermute(value, axis, [(i, i ^ mask) for i in range(count)])


def swap_next(value, axis):
    count = lax.axis_size(axis)
    return lax.ppermute(value, axis, [(i, (i + (1 if i % 2 else -1)) % count) for i in range(count)])


def swap_rows(value):
    bands, sectors = lax.axis_size("lat"), lax.axis_size("lon")
    pairs = []
    for band in range(bands):
        for sector in range(sectors):
            if band == 0 or band == bands - 1:
                other = (band, (sector + sectors // 2) % sectors)
            else:
                other = (band + (1 if band % 2 else -1), sector)
            pairs.append((band * sectors + sector, other[0] * sectors + other[1]))
    return lax.ppermute(value, ("lat", "lon"), pairs)


def local(inputs, kernel, cotangent):
    rows, cols, width = inputs.shape
    bands, sectors = lax.axis_size("lat"), lax.axis_size("lon")

    band, mine, _ = spot()
    odd = band & 1
    half_rows = 9 * width // 2
    unit = 16 * bands
    upper = half_rows * 9 // 16 // unit * unit
    lower = half_rows - upper
    upper_part, lower_part = upper // bands, lower // 2
    upper_end, lower_end = upper_part // 2, lower_part // bands
    first_sizes = [upper_part] * bands + [lower_part] * 2

    def first_rows(band, mine, place):
        rows = [(band ^ m) * upper_part for m in range(bands)]
        rows += [upper + p * lower_part for p in (place, 1 - place)]
        return [mine * half_rows + row for row in rows] + rows

    def upper_rows(band, mine, place):
        return [p * upper_end for _ in range(bands) for p in (place, 1 - place)]

    def lower_rows(band, mine, place):
        return [(band ^ m) * lower_end for _ in range(2) for m in range(bands)]

    def homes(*flips):
        def rows(band, mine, place):
            return [
                (mine ^ h) * half_rows + row
                for h, p in flips
                for m in range(bands)
                for row in (
                    (band ^ m) * upper_part + (place ^ p) * upper_end,
                    upper + (place ^ p) * lower_part + (band ^ m) * lower_end,
                )
            ]

        return rows

    def poles():
        band = lax.axis_index("lat")
        return jnp.where(band == 0, 2, 0), jnp.where(band == bands - 1, 0, 2)

    facts = dict(
        even_band=odd == 0,
        even_sector=mine == 0,
        near_row=(1 - odd) * (rows - 1),
        far_row=odd * (rows - 1),
    )
    inputs, kernel, cotangent, facts = lax.optimization_barrier((inputs, kernel, cotangent, facts))
    even_band, even_sector = facts["even_band"], facts["even_sector"]

    near, far = (
        jnp.stack([lax.dynamic_index_in_dim(field, facts[name], 0, False) for field in (inputs, cotangent)])
        for name in ("near_row", "far_row")
    )
    near = swap(near, "lat", 1)
    far = swap_rows(far)
    columns, window, turned, middle, cot = begin(in_hbm(inputs), in_hbm(cotangent))
    ends = jnp.stack([jnp.where(even_band, far, near), jnp.where(even_band, near, far)], 1)

    def side(place):
        column = 0 if place == 0 else cols - 1
        return jnp.stack(
            [
                jnp.concatenate([ends[k, :1, column], columns[2 * k + place], ends[k, 1:, column]], 0)
                for k in range(2)
            ]
        )

    first, last = side(0), side(1)
    near = swap(jnp.where(even_sector, last, first), "lon", 1)
    far = swap_next(jnp.where(even_sector, first, last), "lon")
    outer = all_taps(window, turned, middle, rows, padded_width(cols))
    sides = jnp.stack([jnp.where(even_sector, far, near), jnp.where(even_sector, near, far)], 1)

    edge_rows = jnp.stack([cotangent[0], cotangent[-1]])
    send, every = with_edges(outer, ends[0], sides[0], edge_rows, columns[2:])

    weights = kernel.reshape(3, 3 * width, width)
    flipped = flip(kernel)
    window = patch(window, ends[0], sides[0])
    cot_window = prepare(cot, ends[1], sides[1])
    flush = Flush()
    for name, (start, count) in pieces(rows):
        if name.startswith("forward"):
            conv(None, window, weights, inputs.shape, start, count, "outputs", flush)
        else:
            conv(poles, cot_window, flipped, inputs.shape, start, count, "input_grad", flush)

    got = swap(send, "lon", 1)
    *parts, low_keep, low_send = add_blocks(first_rows, [every, got], first_sizes)
    low_got = swap(low_send, "lon", 2)
    got = []
    for m in range(1, bands):
        got.append(swap(parts[m], "lat", m))
    lows = add_blocks(lower_rows, [low_keep, low_got], [lower_end] * bands)
    keep, send = add_blocks(upper_rows, [parts[0], *got], [upper_end] * 2)
    low_got = []
    got = swap(send, "lon", 2)
    for m in range(1, bands):
        low_got.append(swap(lows[m], "lat", m))
    value = join_sums([keep, got], [lows[0], *low_got])
    factor = 1.0 / math.sqrt(rows * cols * bands * sectors)
    mask = 4
    while mask < sectors:
        terms = [value, swap(value, "lon", mask)]
        mask *= 2
        if mask < sectors:
            value = terms[0] + terms[1]

    coded = last_sum(terms, factor).astype(HALF)
    other = swap(coded, "lon", 2)
    whole, cuts = 9 * width, (upper_end, lower_end)

    def spread(value):
        got = []
        for m in range(1, bands):
            got.append(swap(value, "lat", m))
        return [value, *got]

    near = spread(coded)
    far = spread(other)
    near = jnp.stack(near)
    near_other = swap(near, "lon", 1)
    near_blocks = decode(near)
    far = jnp.stack(far)
    far_other = swap(far, "lon", 1)
    most = jnp.concatenate([near_blocks, decode(far), decode(near_other)])
    kernel_grad = put_blocks(homes((0, 0), (0, 1), (1, 0)), most, cuts, whole, None, flush, inputs.shape)
    kernel_grad = put_blocks(homes((1, 1)), decode(far_other), cuts, whole, kernel_grad)
    return (flush.outputs["outputs"], flush.outputs["input_grad"], kernel_grad.reshape(3, 3, width, width))


PIECES = (
    ("forward_0", 0, 60),
    ("forward_1", 60, 90),
    ("backward_0", 0, 75),
    ("backward_1", 75, 90),
)


def pieces(rows):
    if max(high for _, _, high in PIECES) != rows:
        return [("forward_0", (0, rows)), ("backward_0", (0, rows))]
    return [(name, (low, high - low)) for name, low, high in PIECES]


def solution(mesh):
    in_specs = (P("lat", "lon", None), P(), P("lat", "lon", None))
    out_specs = (P("lat", "lon", None), P("lat", "lon", None), P())
    return jax.shard_map(local, mesh=mesh, in_specs=in_specs, out_specs=out_specs, check_vma=False)
```

```python
import math

import jax
import jax.numpy as jnp
from jax import lax
from jax.experimental import pallas as pl
from jax.experimental.pallas import tpu as pltpu
from jax.sharding import PartitionSpec as P


F32 = jnp.float32
BF16 = jnp.bfloat16
HALF = jnp.float16
VMEM = pl.BlockSpec(memory_space=pltpu.VMEM)
SMEM = pl.BlockSpec(memory_space=pltpu.SMEM)
HBM = pl.BlockSpec(memory_space=pltpu.HBM)


def padded_width(cols):
    return -(-(cols + 3) // 16) * 16


def in_hbm(value):
    return pltpu.with_memory_space_constraint(value, pltpu.HBM)


def spot():
    sector = lax.axis_index("lon")
    return lax.axis_index("lat"), sector & 1, (sector >> 1) & 1


def params(mib):
    return pltpu.CompilerParams(vmem_limit_bytes=mib << 20)


def shifted(row, left, right, wide):
    cols, width = row.shape
    middle = jnp.zeros((wide - cols - 2, width), F32)
    base = jnp.concatenate([row.astype(F32), right, middle, left], 0)
    return (
        pltpu.roll(base, 1, 0).astype(BF16),
        base.astype(BF16),
        pltpu.roll(base, wide - 1, 0).astype(BF16),
    )


def fill_window(field, ends, sides, side_rows, window, first, rows):
    total, cols, width = field.shape
    wide = padded_width(cols)
    side_rows[...] = sides[...].astype(F32)

    def put(slot, row, at):
        parts = shifted(row, side_rows[0, pl.ds(at, 1)], side_rows[1, pl.ds(at, 1)], wide)
        start = slot * wide if isinstance(slot, int) else pl.multiple_of(slot * wide, 16)
        for tap, part in enumerate(parts):
            window[pl.ds(start, wide), tap * width : (tap + 1) * width] = part

    low = 0
    if first == 0:
        put(0, ends[0], 0)
        low = 1
    high = rows + 2
    if first + rows == total:
        put(rows + 1, ends[1], total + 1)
        high = rows + 1

    @pl.loop(low, high)
    def _(slot):
        put(slot, field[first + slot - 1], first + slot)


def block_rows(rows):
    return max(n for n in range(1, 6) if rows % n == 0)


def conv_rows(taps, window, weights, result, cols, first, rows, total):
    width = weights.shape[-1]
    wide = padded_width(cols)
    step = block_rows(rows)

    def term(slot, count, which):
        at = slot * wide if isinstance(slot, int) else pl.multiple_of(slot * wide, 16)
        return jnp.dot(window[pl.ds(at, count * wide), :], weights[which], preferred_element_type=F32)

    def block(i, top=0, bottom=2):
        start = i * step
        if isinstance(top, int):
            value = term(start, step, 0)
        else:
            value = jnp.concatenate([term(start, 1, top), term(start + 1, step - 1, 0)], 0)
        value = value + term(start + 1, step, 1)
        if isinstance(bottom, int):
            value = value + term(start + 2, step, 2)
        else:
            value = value + jnp.concatenate(
                [term(start + 2, step - 1, 2), term(start + step + 1, 1, bottom)], 0
            )
        result[pl.ds(start, step)] = value.reshape(step, wide, width)[:, :cols].astype(BF16)

    count = rows // step
    poles = taps is not None and step > 1
    low = int(first == 0 and poles)
    high = count - int(first + rows == total and poles)
    group = 3
    trips = (high - low) // group

    @pl.loop(0, trips)
    def _(j):
        for u in range(group):
            block(low + j * group + u)

    for i in range(low + trips * group, high):
        block(i)
    if low:
        block(0, top=taps[0])
    if high < count:
        block(count - 1, bottom=taps[1])


def conv_cost(rows, cols, width):
    wide = padded_width(cols)
    return pl.CostEstimate(
        flops=18 * rows * wide * width * width, bytes_accessed=4 * rows * wide * width, transcendentals=0
    )


def prepare(field, ends, sides):
    total, cols, width = field.shape
    wide = padded_width(cols)

    def body(field, ends, sides, window, side_rows):
        fill_window(field, ends, sides, side_rows, window, 0, total)

    return pl.pallas_call(
        body,
        out_shape=jax.ShapeDtypeStruct(((total + 2) * wide, 3 * width), BF16),
        in_specs=[VMEM] * 3,
        out_specs=VMEM,
        scratch_shapes=[pltpu.VMEM((2, total + 2, width), F32)],
        compiler_params=params(8),
        cost_estimate=pl.CostEstimate(flops=0, bytes_accessed=8 * total * wide * width, transcendentals=0),
    )(field, ends, sides)


def patch(window, ends, sides):
    _, cols, width = ends.shape
    wide = padded_width(cols)
    total = sides.shape[1] - 2

    def body(old, ends, sides, window, side_rows):
        side_rows[...] = sides[...].astype(F32)
        for slot, k in ((0, 0), (total + 1, 1)):
            parts = shifted(ends[k], side_rows[0, slot : slot + 1], side_rows[1, slot : slot + 1], wide)
            for tap, part in enumerate(parts):
                window[slot * wide : (slot + 1) * wide, tap * width : (tap + 1) * width] = part
        place = lax.broadcasted_iota(jnp.int32, (16, width), 0)
        last = (cols - 1) // 16 * 16

        @pl.loop(1, total + 1)
        def _(slot):
            for k, (offset, at) in enumerate(((0, 0), (last, cols - 1 - last))):
                where = (pl.ds(pl.multiple_of(slot * wide + offset, 16), 16), slice(2 * k * width, (2 * k + 1) * width))
                value = window[where].astype(F32)
                window[where] = jnp.where(place == at, side_rows[k, pl.ds(slot, 1)], value).astype(BF16)

    return pl.pallas_call(
        body,
        out_shape=jax.ShapeDtypeStruct(window.shape, BF16),
        in_specs=[VMEM] * 3,
        out_specs=VMEM,
        scratch_shapes=[pltpu.VMEM((2, total + 2, width), F32)],
        input_output_aliases={0: 0},
        compiler_params=params(8),
        cost_estimate=pl.CostEstimate(flops=0, bytes_accessed=256 * total * width, transcendentals=0),
    )(window, ends, sides)


class Flush:
    def __init__(self):
        self.piece = self.first = self.name = None
        self.outputs = {}

    def operands(self):
        if self.piece is None:
            return []
        known = self.outputs.get(self.name)
        return [self.piece] if known is None else [self.piece, known]

    def specs(self):
        return [VMEM, HBM][: len(self.operands())]

    def shapes(self, shape):
        return [] if self.piece is None else [jax.ShapeDtypeStruct(shape, BF16)]

    def aliases(self, operand, output):
        return {operand + 1: output} if len(self.operands()) == 2 else {}

    def scratch(self):
        return [] if self.piece is None else [pltpu.SemaphoreType.DMA]

    def copy(self, piece, out, sem):
        return pltpu.make_async_copy(piece, out.at[pl.ds(self.first, self.piece.shape[0])], sem)


def conv(taps, window, weights, shape, first, rows, name, flush):
    total, cols, width = shape
    wide = padded_width(cols)
    more = flush.operands()
    inputs = 2

    def body(*refs):
        window, weights = refs[:inputs]
        result = refs[inputs + len(more)]
        copy = None
        if more:
            copy = flush.copy(refs[inputs], refs[-2], refs[-1])
            copy.start()
        view = window.at[first * wide : (first + rows + 2) * wide]
        conv_rows(taps and taps(), view, weights, result, cols, first, rows, total)
        if copy is not None:
            copy.wait()

    results = pl.pallas_call(
        body,
        out_shape=[jax.ShapeDtypeStruct((rows, cols, width), BF16)] + flush.shapes(shape),
        in_specs=[VMEM] * 2 + flush.specs(),
        out_specs=[VMEM] + [HBM] * bool(more),
        scratch_shapes=flush.scratch(),
        input_output_aliases=flush.aliases(inputs, 1),
        compiler_params=params(8),
        cost_estimate=conv_cost(rows, cols, width),
    )(window, weights, *more)
    if more:
        flush.outputs[flush.name] = results[1]
    flush.piece, flush.first, flush.name = results[0], first, name


def turn_group(wide):
    return 128 // math.gcd(128, wide)


def begin_kernel(field_hbm, cot_hbm, columns, window, turned, sums, cot, field, column_rows, sems):
    total, cols, width = field.shape
    wide = padded_width(cols)
    part = 3 * turn_group(wide)
    chunks = -(-total // part)
    sizes = [min(part, total - at) for at in range(0, total, part)]

    def copies(i, size):
        at = i * part
        return [
            pltpu.make_async_copy(source.at[pl.ds(at, size)], target.at[pl.ds(at, size)], sems.at[i, j])
            for j, (source, target) in enumerate(((field_hbm, field), (cot_hbm, cot)))
        ]

    for i, size in enumerate(sizes):
        for copy in copies(i, size):
            copy.start()
    empty = jnp.zeros((1, width), F32)
    blank = jnp.zeros((wide - cols, width), F32)
    for k in range(3):
        window[0:wide, k * width : (k + 1) * width] = jnp.zeros((wide, width), BF16)
        window[(total + 1) * wide : (total + 2) * wide, k * width : (k + 1) * width] = jnp.zeros((wide, width), BF16)
    sums[...] = jnp.zeros_like(sums)

    def lay(i, size):
        for copy in copies(i, size):
            copy.wait()
        for low in range(0, size, turn_group(wide)):
            step = min(turn_group(wide), size - low)
            flat = []
            for u in range(low, low + step):
                r = i * part + u
                row, other = field[r], cot[r].astype(F32)
                start = pl.multiple_of((r + 1) * wide, 16)
                for tap, piece in enumerate(shifted(row, empty, empty, wide)):
                    window[pl.ds(start, wide), tap * width : (tap + 1) * width] = piece
                row = row.astype(F32)
                for k, value in enumerate((row[0:1], row[cols - 1 : cols], other[0:1], other[cols - 1 : cols])):
                    column_rows[k, pl.ds(r, 1)] = value
                flat += [other, blank]
            value = jnp.concatenate(flat, 0).T.astype(BF16)
            turned[:, pl.ds(pl.multiple_of((i * part + low) * wide, 128), step * wide)] = value

    def multiply(i, size):
        at = i * part * wide
        at = at if isinstance(at, int) else pl.multiple_of(at, 128)
        sums[...] += jnp.dot(
            turned[:, pl.ds(at, size * wide)],
            window[pl.ds(at + wide, size * wide), :],
            preferred_element_type=F32,
        )

    lay(0, sizes[0])

    @pl.loop(1, chunks - 1)
    def _(i):
        lay(i, part)
        multiply(i - 1, part)

    if chunks > 1:
        lay(chunks - 1, sizes[-1])
        multiply(chunks - 2, part)
    multiply(chunks - 1, sizes[-1])
    columns[...] = column_rows[...].astype(BF16)


def store_turned(value, taps, slot):
    width = taps.shape[-1]
    for b in range(3):
        taps[slot + b] = value[:, b * width : (b + 1) * width].T


def begin(field, cot):
    total, cols, width = field.shape
    wide = padded_width(cols)
    group = turn_group(wide)
    return pl.pallas_call(
        begin_kernel,
        out_shape=(
            jax.ShapeDtypeStruct((4, total, width), BF16),
            jax.ShapeDtypeStruct(((total + 2) * wide, 3 * width), BF16),
            jax.ShapeDtypeStruct((width, -(-total // group) * group * wide), BF16),
            jax.ShapeDtypeStruct((width, 3 * width), F32),
            jax.ShapeDtypeStruct(cot.shape, BF16),
        ),
        in_specs=[HBM, HBM],
        out_specs=(VMEM,) * 5,
        scratch_shapes=[
            pltpu.VMEM(field.shape, BF16),
            pltpu.VMEM((4, total, width), F32),
            pltpu.SemaphoreType.DMA((-(-total // (3 * group)), 2)),
        ],
        compiler_params=params(12),
        cost_estimate=pl.CostEstimate(
            flops=8 * total * wide * width * width, bytes_accessed=4 * total * wide * width, transcendentals=0
        ),
    )(field, cot)


def flip(kernel):
    width = kernel.shape[-1]

    def body(kernel, out):
        for tap in range(9):
            a, b = divmod(tap, 3)
            out[a, b * width : (b + 1) * width] = kernel[2 - a, 2 - b].astype(F32).T.astype(BF16)

    return pl.pallas_call(
        body,
        out_shape=jax.ShapeDtypeStruct((3, 3 * width, width), BF16),
        in_specs=[VMEM],
        out_specs=VMEM,
        compiler_params=params(8),
        cost_estimate=pl.CostEstimate(flops=0, bytes_accessed=36 * width * width, transcendentals=0),
    )(kernel)


def all_taps(window, turned, middle, total, wide):
    width = turned.shape[0]
    cells = total * wide

    def body(window, turned, middle, taps):
        store_turned(middle[...], taps, 3)
        for slot, start in ((0, 0), (6, 2 * wide)):
            store_turned(
                jnp.dot(turned[:, :cells], window[start : start + cells, :], preferred_element_type=F32), taps, slot
            )

    return pl.pallas_call(
        body,
        out_shape=jax.ShapeDtypeStruct((9, width, width), F32),
        in_specs=[VMEM] * 3,
        out_specs=VMEM,
        compiler_params=params(8),
        cost_estimate=pl.CostEstimate(
            flops=12 * total * wide * width * width, bytes_accessed=4 * total * wide * width, transcendentals=0
        ),
    )(window, turned, middle)


def edge_kernel(taps, ends, sides, rows, columns, send_upper, send_lower, every, side_rows):
    _, cols, width = ends.shape
    wide = padded_width(cols)
    total = columns.shape[1]
    tall = -(-total // 16) * 16
    side_rows[...] = sides[...].astype(F32)
    empty = jnp.zeros((1, width), F32)
    end_parts = [shifted(ends[k], empty, empty, wide) for k in range(2)]
    blank = jnp.zeros((wide - cols, width), F32)
    row_parts = [jnp.concatenate([rows[k].astype(F32), blank], 0).astype(BF16) for k in range(2)]
    low = jnp.zeros((tall - total, width), F32)
    column_parts = [jnp.concatenate([columns[k].astype(F32), low], 0).astype(BF16) for k in range(2)]
    size = 9 * width // 2
    for tap in range(9):
        a, b = divmod(tap, 3)
        left, right = [], []
        if b != 1:
            side = b // 2
            left.append(jnp.concatenate([side_rows[side, a : a + total], low], 0).astype(BF16))
            right.append(column_parts[side])
        if a != 1:
            left.append(end_parts[a // 2][b])
            right.append(row_parts[a // 2])
        value = taps[tap]
        if left:
            value = value + lax.dot_general(
                jnp.concatenate(left, 0),
                jnp.concatenate(right, 0),
                (((0,), (0,)), ((), ())),
                preferred_element_type=F32,
            )
        every[tap * width : (tap + 1) * width] = value
    at = (1 - spot()[1]) * size
    for send in (send_upper, send_lower):
        send[...] = every[pl.ds(pl.multiple_of(at, 8), send.shape[0])]
        at = at + send.shape[0]


def with_edges(taps, ends, sides, rows, columns, upper):
    _, _, width = ends.shape
    total = columns.shape[1]
    return pl.pallas_call(
        edge_kernel,
        out_shape=(
            jax.ShapeDtypeStruct((upper, width), F32),
            jax.ShapeDtypeStruct((9 * width // 2 - upper, width), F32),
            jax.ShapeDtypeStruct((9 * width, width), F32),
        ),
        in_specs=[VMEM] * 5,
        out_specs=(VMEM,) * 3,
        scratch_shapes=[pltpu.VMEM((2, total + 2, width), F32)],
        compiler_params=params(12),
        cost_estimate=pl.CostEstimate(
            flops=16 * 144 * width * width, bytes_accessed=72 * width * width, transcendentals=0
        ),
    )(taps, ends, sides, rows, columns)


def add_blocks(places, terms, sizes):
    width = terms[0].shape[1]
    count = len(sizes)

    def body(*refs):
        where = places(*spot())
        sources, outs = refs[: len(terms)], refs[len(terms) :]
        for k, size in enumerate(sizes):
            value = None
            for t, source in enumerate(sources):
                part = source[pl.ds(pl.multiple_of(where[t * count + k], 8), size)]
                value = part if value is None else value + part
            outs[k][...] = value

    return pl.pallas_call(
        body,
        out_shape=tuple(jax.ShapeDtypeStruct((size, width), F32) for size in sizes),
        in_specs=[VMEM] * len(terms),
        out_specs=(VMEM,) * count,
        compiler_params=params(8),
        cost_estimate=pl.CostEstimate(
            flops=sum(sizes) * width, bytes_accessed=4 * sum(sizes) * width * (len(terms) + 1), transcendentals=0
        ),
    )(*terms)


def join_sums(upper, lower):
    above, width = upper[0].shape
    below = lower[0].shape[0]

    def body(*refs):
        out = refs[-1]
        for at, size, sources in ((0, above, refs[: len(upper)]), (above, below, refs[len(upper) : -1])):
            value = sources[0][...]
            for source in sources[1:]:
                value = value + source[...]
            out[at : at + size] = value

    return pl.pallas_call(
        body,
        out_shape=jax.ShapeDtypeStruct((above + below, width), F32),
        in_specs=[VMEM] * (len(upper) + len(lower)),
        out_specs=VMEM,
        compiler_params=params(8),
        cost_estimate=pl.CostEstimate(
            flops=4 * (above + below) * width, bytes_accessed=16 * (above + below) * width, transcendentals=0
        ),
    )(*upper, *lower)


def last_sum(terms, scale):
    rows, width = terms[0].shape

    def body(first, second, out):
        value = (first[...] + second[...]) * scale
        top = jnp.max(jnp.max(jnp.abs(value), axis=1, keepdims=True), axis=0, keepdims=True)
        exponent = jnp.ceil(jnp.log2(jnp.maximum(top, 1e-37)))
        out[:rows] = value * jnp.exp2(-exponent)
        out[rows:] = jnp.broadcast_to(exponent, (8, width))

    return pl.pallas_call(
        body,
        out_shape=jax.ShapeDtypeStruct((rows + 8, width), F32),
        in_specs=[VMEM] * 2,
        out_specs=VMEM,
        compiler_params=params(8),
        cost_estimate=pl.CostEstimate(flops=8 * rows * width, bytes_accessed=12 * rows * width, transcendentals=0),
    )(*terms)


def decode(coded):
    return coded[..., :-8, :].astype(F32) * jnp.exp2(coded[..., -1:, :].astype(F32))


def put_blocks(places, blocks, cuts, total, out=None, flush=None, shape=None):
    count, _, width = blocks.shape
    more = [] if out is None else [out]
    late = [] if flush is None else flush.operands()
    inputs = 1 + len(more)

    def body(blocks, *rest):
        where = places(*spot())
        refs = rest[len(more) + len(late) :]
        out, sem = refs[0], refs[-1]
        copy = None
        if late:
            copy = flush.copy(rest[len(more)], refs[1], refs[2])
            copy.start()
        for k in range(count):
            start = 0
            for j, size in enumerate(cuts):
                at = pl.multiple_of(where[2 * k + j], 8)
                pltpu.make_async_copy(blocks.at[k, pl.ds(start, size)], out.at[pl.ds(at, size)], sem).start()
                start += size
        pltpu.make_async_copy(blocks, blocks, sem).wait()
        if copy is not None:
            copy.wait()

    results = pl.pallas_call(
        body,
        out_shape=[jax.ShapeDtypeStruct((total, width), F32)] + (flush.shapes(shape) if late else []),
        in_specs=[VMEM] + [HBM] * len(more) + (flush.specs() if late else []),
        out_specs=[HBM] * (1 + bool(late)),
        scratch_shapes=(flush.scratch() if late else []) + [pltpu.SemaphoreType.DMA],
        input_output_aliases={**({1: 0} if more else {}), **(flush.aliases(inputs, 1) if late else {})},
        compiler_params=params(8),
    )(blocks, *more, *late)
    if late:
        flush.outputs[flush.name] = results[1]
    return results[0]


def swap(value, axis, mask):
    count = lax.axis_size(axis)
    return lax.ppermute(value, axis, [(i, i ^ mask) for i in range(count)])


def swap_next(value, axis):
    count = lax.axis_size(axis)
    return lax.ppermute(value, axis, [(i, (i + (1 if i % 2 else -1)) % count) for i in range(count)])


def swap_rows(value):
    bands, sectors = lax.axis_size("lat"), lax.axis_size("lon")
    pairs = []
    for band in range(bands):
        for sector in range(sectors):
            if band == 0 or band == bands - 1:
                other = (band, (sector + sectors // 2) % sectors)
            else:
                other = (band + (1 if band % 2 else -1), sector)
            pairs.append((band * sectors + sector, other[0] * sectors + other[1]))
    return lax.ppermute(value, ("lat", "lon"), pairs)


def local(inputs, kernel, cotangent):
    rows, cols, width = inputs.shape
    bands, sectors = lax.axis_size("lat"), lax.axis_size("lon")

    band, mine, _ = spot()
    odd = band & 1
    half_rows = 9 * width // 2
    unit = 16 * bands
    upper = half_rows // 2 // unit * unit
    lower = half_rows - upper
    upper_part, lower_part = upper // bands, lower // 2
    upper_end, lower_end = upper_part // 2, lower_part // bands

    def first_upper(band, mine, place):
        rows = [(band ^ m) * upper_part for m in range(bands)]
        return [mine * half_rows + row for row in rows] + rows

    def first_lower(band, mine, place):
        rows = [p * lower_part for p in (place, 1 - place)]
        return [mine * half_rows + upper + row for row in rows] + rows

    def upper_rows(band, mine, place):
        return [p * upper_end for _ in range(bands) for p in (place, 1 - place)]

    def lower_rows(band, mine, place):
        return [(band ^ m) * lower_end for _ in range(2) for m in range(bands)]

    def homes(*flips):
        def rows(band, mine, place):
            return [
                (mine ^ h) * half_rows + row
                for h, p in flips
                for m in range(bands)
                for row in (
                    (band ^ m) * upper_part + (place ^ p) * upper_end,
                    upper + (place ^ p) * lower_part + (band ^ m) * lower_end,
                )
            ]

        return rows

    def poles():
        band = lax.axis_index("lat")
        return jnp.where(band == 0, 2, 0), jnp.where(band == bands - 1, 0, 2)

    facts = dict(
        even_band=odd == 0,
        even_sector=mine == 0,
        near_row=(1 - odd) * (rows - 1),
        far_row=odd * (rows - 1),
    )
    inputs, kernel, cotangent, facts = lax.optimization_barrier((inputs, kernel, cotangent, facts))
    even_band, even_sector = facts["even_band"], facts["even_sector"]

    near, far = (
        jnp.stack([lax.dynamic_index_in_dim(field, facts[name], 0, False) for field in (inputs, cotangent)])
        for name in ("near_row", "far_row")
    )
    near = swap(near, "lat", 1)
    far = swap_rows(far)
    columns, window, turned, middle, cot = begin(in_hbm(inputs), in_hbm(cotangent))
    ends = jnp.stack([jnp.where(even_band, far, near), jnp.where(even_band, near, far)], 1)

    def side(place):
        column = 0 if place == 0 else cols - 1
        return jnp.stack(
            [
                jnp.concatenate([ends[k, :1, column], columns[2 * k + place], ends[k, 1:, column]], 0)
                for k in range(2)
            ]
        )

    first, last = side(0), side(1)
    near = swap(jnp.where(even_sector, last, first), "lon", 1)
    far = swap_next(jnp.where(even_sector, first, last), "lon")
    outer = all_taps(window, turned, middle, rows, padded_width(cols))
    sides = jnp.stack([jnp.where(even_sector, far, near), jnp.where(even_sector, near, far)], 1)

    edge_rows = jnp.stack([cotangent[0], cotangent[-1]])
    send_upper, send_lower, every = with_edges(outer, ends[0], sides[0], edge_rows, columns[2:], upper)

    weights = kernel.reshape(3, 3 * width, width)
    flipped = flip(kernel)
    window = patch(window, ends[0], sides[0])
    cot_window = prepare(cot, ends[1], sides[1])
    flush = Flush()
    for name, (start, count) in pieces(rows):
        if name.startswith("forward"):
            conv(None, window, weights, inputs.shape, start, count, "outputs", flush)
        else:
            conv(poles, cot_window, flipped, inputs.shape, start, count, "input_grad", flush)

    got = swap(send_lower, "lon", 1)
    low_keep, low_send = add_blocks(first_lower, [every, got], [lower_part] * 2)
    got = swap(send_upper, "lon", 1)
    parts = add_blocks(first_upper, [every, got], [upper_part] * bands)
    low_got = swap(low_send, "lon", 2)
    got = []
    for m in range(1, bands):
        got.append(swap(parts[m], "lat", m))
    lows = add_blocks(lower_rows, [low_keep, low_got], [lower_end] * bands)
    keep, send = add_blocks(upper_rows, [parts[0], *got], [upper_end] * 2)
    low_got = []
    got = swap(send, "lon", 2)
    for m in range(1, bands):
        low_got.append(swap(lows[m], "lat", m))
    value = join_sums([keep, got], [lows[0], *low_got])
    factor = 1.0 / math.sqrt(rows * cols * bands * sectors)
    mask = 4
    while mask < sectors:
        terms = [value, swap(value, "lon", mask)]
        mask *= 2
        if mask < sectors:
            value = terms[0] + terms[1]

    coded = last_sum(terms, factor).astype(HALF)
    other = swap(coded, "lon", 2)
    whole, cuts = 9 * width, (upper_end, lower_end)

    def spread(value):
        got = []
        for m in range(1, bands):
            got.append(swap(value, "lat", m))
        return [value, *got]

    near = spread(coded)
    far = spread(other)
    near = jnp.stack(near)
    near_other = swap(near, "lon", 1)
    near_blocks = decode(near)
    far = jnp.stack(far)
    far_other = swap(far, "lon", 1)
    most = jnp.concatenate([near_blocks, decode(far), decode(near_other)])
    kernel_grad = put_blocks(homes((0, 0), (0, 1), (1, 0)), most, cuts, whole, None, flush, inputs.shape)
    kernel_grad = put_blocks(homes((1, 1)), decode(far_other), cuts, whole, kernel_grad)
    return (flush.outputs["outputs"], flush.outputs["input_grad"], kernel_grad.reshape(3, 3, width, width))


PIECES = (
    ("forward_0", 0, 60),
    ("forward_1", 60, 90),
    ("backward_0", 0, 75),
    ("backward_1", 75, 90),
)


def pieces(rows):
    if max(high for _, _, high in PIECES) != rows:
        return [("forward_0", (0, rows)), ("backward_0", (0, rows))]
    return [(name, (low, high - low)) for name, low, high in PIECES]


def solution(mesh):
    in_specs = (P("lat", "lon", None), P(), P("lat", "lon", None))
    out_specs = (P("lat", "lon", None), P("lat", "lon", None), P())
    return jax.shard_map(local, mesh=mesh, in_specs=in_specs, out_specs=out_specs, check_vma=False)
```
